32 devices in a mesh: groups: 2 (over x), seq: 8 (over z, y), tp: 2 (over core).
Axes of the slice: x: 2, y: 2, z: 4, core: 2. Of those that a mesh axis runs over, the one named last changes fastest.
Arguments:
- queries: bfloat16 [4096, 8192], P(('groups', 'seq', 'tp')), parts along dimension 0, may hold values from -10 to 10
- keys: bfloat16 [4096, 1024], P(('groups', 'seq', 'tp')), parts along dimension 0, may hold values from -10 to 10
- values: bfloat16 [4096, 1024], P(('groups', 'seq', 'tp')), parts along dimension 0, may hold values from -6 to 6
- vertical_blocks: int32 [64, 2], replicated, may hold values from 0 to 15, as said below
- vertical_count: int32 [64], replicated, may hold values from 1 to 2, as said below
- slash_offsets: int32 [64, 2], replicated, may hold values from 1 to 15, as said below
- slash_count: int32 [64], replicated, may hold values from 1 to 2, as said below
Outputs:
- attention: bfloat16 [4096, 8192], P(('groups', 'seq', 'tp')), parts along dimension 0
The draws below stay inside these ranges and needn't reach their ends.
There are 2 independent parts, one for each index of `groups`. The reference program is written for one: setup_inputs(seed, part) draws one part's arguments, and reference() takes and returns one part's arrays. A program takes and returns all parts, laid end to end along the dimension named above; an argument that names none is the same for every part. Nothing has to cross between parts.
Inputs may be any that keep to these rules, and one draw needn't show every extreme that they name: `vertical_blocks`: the 2 entries of one head are distinct. `vertical_count`: some head uses all 2 entries. `slash_offsets`: the 2 entries of one head are distinct. `slash_count`: some head uses all 2 entries.
All inputs are finite; a program needn't handle non-finite values.
Results may differ from the reference program's by a relative error of at most 0.0037.
Values may be sent and summed in bfloat16 or wider, within the bound.
No kernel may reach another device: no remote copies, remote signals or barrier semaphores. Data moves between devices by JAX's collectives and lax.ppermute only.
A program may use at most 128 MiB of HBM per device.

```python
import jax
import jax.numpy as jnp
from jax import lax

QUERY_HEADS = 64
KEY_VALUE_HEADS = 8
HEAD_SIZE = 128
MASK_BLOCK_SIZE = 128
NVMAX = 2
NSMAX = 2
SEQUENCE_LENGTH = 2048


def paired_draw(key):
    start_offset = jax.random.fold_in(key, 11)
    query_portion = jax.random.normal(jax.random.fold_in(start_offset, 1), (SEQUENCE_LENGTH, QUERY_HEADS, HEAD_SIZE), jnp.float32)
    key_portion = jax.random.normal(jax.random.fold_in(start_offset, 2), (SEQUENCE_LENGTH, KEY_VALUE_HEADS, HEAD_SIZE), jnp.float32)
    return (query_portion.reshape(SEQUENCE_LENGTH, QUERY_HEADS * HEAD_SIZE), key_portion.reshape(SEQUENCE_LENGTH, KEY_VALUE_HEADS * HEAD_SIZE))


def draw_queries(key, part):
    return paired_draw(key)[0].astype(jnp.bfloat16)


def draw_keys(key, part):
    return paired_draw(key)[1].astype(jnp.bfloat16)


def draw_vertical_blocks(key, part):
    head_keys = jax.random.split(jax.random.fold_in(key, 21), QUERY_HEADS)
    picked = jax.vmap(lambda one_key: jax.random.permutation(one_key, SEQUENCE_LENGTH // MASK_BLOCK_SIZE)[:NVMAX])(head_keys)
    return picked.astype(jnp.int32)


def draw_vertical_count(key, part):
    counts = jax.random.randint(jax.random.fold_in(key, 22), (QUERY_HEADS,), 1, NVMAX + 1)
    fullest = jax.random.randint(jax.random.fold_in(key, 23), (), 0, QUERY_HEADS)
    return counts.at[fullest].set(NVMAX).astype(jnp.int32)


def draw_slash_offsets(key, part):
    head_keys = jax.random.split(jax.random.fold_in(key, 31), QUERY_HEADS)
    picked = jax.vmap(lambda one_key: jax.random.permutation(one_key, SEQUENCE_LENGTH // MASK_BLOCK_SIZE - 1)[:NSMAX] + 1)(head_keys)
    return picked.astype(jnp.int32)


def draw_slash_count(key, part):
    counts = jax.random.randint(jax.random.fold_in(key, 32), (QUERY_HEADS,), 1, NSMAX + 1)
    fullest = jax.random.randint(jax.random.fold_in(key, 33), (), 0, QUERY_HEADS)
    return counts.at[fullest].set(NSMAX).astype(jnp.int32)


def steps_of(own_key, shape, cuts, low, top_value):
    def one(dim, parts):
        draws = jax.random.uniform(jax.random.fold_in(jax.random.fold_in(own_key, 6), dim), (parts,), jnp.float32, low / len(cuts), top_value / len(cuts))
        return jnp.repeat(jnp.exp(draws), shape[dim] // parts).reshape((-1,) + (1,) * (len(shape) - dim - 1))

    level = one(*cuts[0])
    for cut in cuts[1:]:
        level = level * one(*cut)
    return level


def gaussian(own_key, shape, spread, limit, cuts=(), held_as=jnp.bfloat16):
    gain = steps_of(own_key, shape, cuts, -0.22, 0.18) if cuts else 1.0
    values = jax.random.normal(own_key, shape, jnp.float32) * spread * gain
    return jnp.minimum(jnp.maximum(values, -limit), limit).astype(held_as)


def setup_inputs(seed: int = 0, part: int = 0) -> dict:
    seeds = jax.random.split(jax.random.key(seed), 8)
    part_splits = jax.random.split(jax.random.fold_in(seeds[7], part), 8)
    queries = draw_queries(jax.random.fold_in(jax.random.fold_in(seeds[7], part), 71), part)
    keys = draw_keys(jax.random.fold_in(jax.random.fold_in(seeds[7], part), 71), part)
    values = gaussian(part_splits[2], (SEQUENCE_LENGTH, KEY_VALUE_HEADS * HEAD_SIZE), 1.0, 6.0, ((0, 16),))
    vertical_blocks = draw_vertical_blocks(jax.random.fold_in(seeds[7], 71), part)
    vertical_count = draw_vertical_count(jax.random.fold_in(seeds[7], 71), part)
    slash_offsets = draw_slash_offsets(jax.random.fold_in(seeds[7], 71), part)
    slash_count = draw_slash_count(jax.random.fold_in(seeds[7], 71), part)
    return {"queries": queries, "keys": keys, "values": values, "vertical_blocks": vertical_blocks, "vertical_count": vertical_count, "slash_offsets": slash_offsets, "slash_count": slash_count}


def head_attend(query_blocks, block_index, row_offset, key_blocks, value_blocks, verticals, vertical_live, slash_list, slash_live):
    query_rows = query_blocks.shape[1]
    scaling = query_blocks.shape[2] ** -0.5
    total_block_count = key_blocks.shape[0]
    block_width = key_blocks.shape[1]
    block_total = block_index.shape[0]
    vertical_entries = jnp.arange(verticals.shape[0])
    slash_entries = jnp.arange(slash_list.shape[0])
    member = jnp.any((jnp.arange(total_block_count)[:, None] == verticals[None, :]) & (vertical_entries < vertical_live)[None, :], axis=1)
    vertical_active = (block_index[:, None] > verticals[None, :]) & (vertical_entries < vertical_live)[None, :]
    targets = block_index[:, None] - slash_list[None, :]
    safe_targets = jnp.clip(targets, 0, total_block_count - 1)
    slash_active = (targets >= 0) & (slash_entries < slash_live)[None, :] & jnp.logical_not(jnp.take(member, safe_targets))
    tile_index = jnp.concatenate([block_index[:, None],
                                  jnp.broadcast_to(verticals[None, :], (block_total, verticals.shape[0])),
                                  safe_targets], axis=1).astype(jnp.int32)
    tile_active = jnp.concatenate([jnp.ones((block_total, 1), bool), vertical_active, slash_active], axis=1)
    tile_keys = jnp.take(key_blocks, tile_index, axis=0).astype(jnp.float32)
    tile_values = jnp.take(value_blocks, tile_index, axis=0).astype(jnp.float32)
    scores = jnp.einsum("nqd,ntkd->nqtk", query_blocks.astype(jnp.float32), tile_keys) * scaling
    query_pos = row_offset + jnp.arange(query_rows)
    causal = query_pos[:, None] >= jnp.arange(block_width)[None, :]
    off_diagonal = (jnp.arange(tile_index.shape[1]) > 0)[None, None, :, None]
    allowed = tile_active[:, None, :, None] & (causal[None, :, None, :] | off_diagonal)
    scores = jnp.where(allowed, scores, -jnp.inf)
    peak = jnp.max(scores, axis=(2, 3))
    weights = jnp.exp(scores - peak[:, :, None, None])
    total = jnp.sum(weights, axis=(2, 3))
    rounded = lax.optimization_barrier(weights.astype(jnp.bfloat16)).astype(jnp.float32)
    numerator = jnp.einsum("nqtk,ntkd->nqd", rounded, tile_values)
    return (numerator / total[..., None]).astype(jnp.bfloat16)


def reference(queries, keys, values, vertical_blocks, vertical_count, slash_offsets, slash_count):
    total_block_count = SEQUENCE_LENGTH // MASK_BLOCK_SIZE
    heads_per_group = QUERY_HEADS // KEY_VALUE_HEADS
    query_heads = queries.reshape(total_block_count, MASK_BLOCK_SIZE, QUERY_HEADS, HEAD_SIZE)
    heads_of_keys = keys.reshape(total_block_count, MASK_BLOCK_SIZE, KEY_VALUE_HEADS, HEAD_SIZE)
    heads_of_values = values.reshape(total_block_count, MASK_BLOCK_SIZE, KEY_VALUE_HEADS, HEAD_SIZE)
    block_index = jnp.arange(total_block_count, dtype=jnp.int32)

    def one_head(head):
        query_blocks = lax.dynamic_index_in_dim(query_heads, head, 2, False)
        kv_head = head // heads_per_group
        key_blocks = lax.dynamic_index_in_dim(heads_of_keys, kv_head, 2, False)
        value_blocks = lax.dynamic_index_in_dim(heads_of_values, kv_head, 2, False)
        return head_attend(query_blocks, block_index, 0, key_blocks, value_blocks,
                           vertical_blocks[head], vertical_count[head], slash_offsets[head], slash_count[head])

    outputs = lax.map(one_head, jnp.arange(QUERY_HEADS, dtype=jnp.int32))
    return jnp.transpose(outputs, (1, 2, 0, 3)).reshape(SEQUENCE_LENGTH, QUERY_HEADS * HEAD_SIZE)
```

```python
import functools

import jax
import jax.numpy as jnp
from jax import lax
from jax.experimental import pallas as pl
from jax.experimental.pallas import tpu as pltpu
from jax.sharding import PartitionSpec as P

QUERY_HEADS = 64
KEY_VALUE_HEADS = 8
HEAD_SIZE = 128
MASK_BLOCK_SIZE = 128
GROUP = QUERY_HEADS // KEY_VALUE_HEADS
LOG2E = 1.4426950408889634


def attend_kernel(geometry, table, own_queries, sibling_queries, *refs):
    relay, columns, cores, kv_first, vertical_width, slash_width, offsets, pieces = geometry
    piece_refs = refs[: len(pieces)]
    own_out, sibling_out, key_rows, value_rows = refs[len(pieces) :]
    chip_rows = cores * MASK_BLOCK_SIZE
    step = pl.program_id(0)
    vertical_at, vertical_count_at, slash_at, slash_count_at, rank_at, core_at = offsets
    rank = table[rank_at]
    core = table[core_at]
    kv_head = core * (KEY_VALUE_HEADS // cores) + kv_first + step

    @pl.when(step == 0)
    def _():
        value_rows[:, HEAD_SIZE:] = jnp.ones((value_rows.shape[0], HEAD_SIZE), jnp.bfloat16)

    for ref, (chips, slots) in zip(piece_refs, pieces):
        for chip in range(chips):
            rows = pl.ds(slots[chip] * chip_rows, chip_rows)
            key_rows[rows, :] = ref[chip, 0, 0]
            value_rows[rows, :HEAD_SIZE] = ref[chip, 0, 1]

    causal = lax.broadcasted_iota(jnp.int32, (MASK_BLOCK_SIZE, MASK_BLOCK_SIZE), 0) >= lax.broadcasted_iota(
        jnp.int32, (MASK_BLOCK_SIZE, MASK_BLOCK_SIZE), 1
    )
    factor = HEAD_SIZE**-0.5 * LOG2E
    own_slot = 0 if relay else rank

    def row_of(block):
        chip = block // cores
        if relay:
            slot = (rank // columns - chip // columns) * columns + jnp.bitwise_xor(rank % columns, chip % columns)
        else:
            slot = chip
        return (slot * cores + jnp.bitwise_xor(block % cores, core)) * MASK_BLOCK_SIZE

    def unit(queries, block, diagonal_row, head):
        rows = [diagonal_row]
        active = [None]
        verticals = []
        for entry in range(vertical_width):
            vertical = table[vertical_at + head * vertical_width + entry]
            live = entry < table[vertical_count_at + head]
            verticals.append((vertical, live))
            use = live & (vertical < block)
            rows.append(row_of(jnp.where(use, vertical, block)))
            active.append(use)
        for entry in range(slash_width):
            target = block - table[slash_at + head * slash_width + entry]
            use = (entry < table[slash_count_at + head]) & (target >= 0)
            for vertical, live in verticals:
                use = use & jnp.logical_not(live & (vertical == target))
            rows.append(row_of(jnp.where(use, target, block)))
            active.append(use)
        rows = [pl.multiple_of(row, MASK_BLOCK_SIZE) for row in rows]
        keys = jnp.concatenate([key_rows[pl.ds(row, MASK_BLOCK_SIZE), :] for row in rows], axis=0)
        values = jnp.concatenate([value_rows[pl.ds(row, MASK_BLOCK_SIZE), :] for row in rows], axis=0)
        scores = lax.dot_general(queries, keys, (((1,), (1,)), ((), ())), preferred_element_type=jnp.float32)
        tiles = []
        for index, use in enumerate(active):
            tile = scores[:, index * MASK_BLOCK_SIZE : (index + 1) * MASK_BLOCK_SIZE]
            tiles.append(jnp.where(causal if use is None else use, tile, -jnp.inf))
        peak = functools.reduce(jnp.maximum, tiles)
        peak = jnp.max(peak, axis=1, keepdims=True)
        weights = [jnp.exp2((tile - peak) * factor).astype(jnp.bfloat16) for tile in tiles]
        sums = jnp.dot(jnp.concatenate(weights, axis=1), values, preferred_element_type=jnp.float32)
        return (sums[:, :HEAD_SIZE] / sums[:, HEAD_SIZE:]).astype(jnp.bfloat16)

    def head_pair(slot, carry):
        head = kv_head * GROUP + slot
        lanes = pl.ds(pl.multiple_of(slot * HEAD_SIZE, HEAD_SIZE), HEAD_SIZE)
        base = own_slot * chip_rows
        own_out[:, lanes] = unit(own_queries[:, lanes], rank * cores + core, base, head)
        sibling_out[:, lanes] = unit(
            sibling_queries[:, lanes], rank * cores + (cores - 1 - core), base + MASK_BLOCK_SIZE, head
        )
        return carry

    lax.fori_loop(0, GROUP, head_pair, 0, unroll=2)


def attend(table, geometry, queries, sibling_queries, pieces, kv_heads):
    _, _, cores, kv_first, _, _, offsets, layout = geometry
    tokens = queries.shape[0]
    width = GROUP * HEAD_SIZE
    core_at = offsets[-1]
    half = KEY_VALUE_HEADS // cores
    chip_rows = cores * MASK_BLOCK_SIZE
    rows = sum(chips for chips, _ in layout) * chip_rows

    def piece_spec(piece):
        return pl.BlockSpec((piece.shape[0], 1, 2, chip_rows, HEAD_SIZE), lambda g, t: (0, g, 0, 0, 0))

    return pl.pallas_call(
        functools.partial(attend_kernel, geometry),
        grid_spec=pltpu.PrefetchScalarGridSpec(
            num_scalar_prefetch=1,
            grid=(kv_heads,),
            in_specs=[
                pl.BlockSpec((tokens, width), lambda g, t: (0, t[core_at] * half + kv_first + g)),
                pl.BlockSpec((tokens, width), lambda g, t: (0, kv_first + g)),
            ]
            + [piece_spec(piece) for piece in pieces],
            out_specs=[
                pl.BlockSpec((tokens, width), lambda g, t: (0, g)),
                pl.BlockSpec((tokens, width), lambda g, t: (0, g)),
            ],
            scratch_shapes=[
                pltpu.VMEM((rows, HEAD_SIZE), jnp.bfloat16),
                pltpu.VMEM((rows, 2 * HEAD_SIZE), jnp.bfloat16),
            ],
        ),
        out_shape=[jax.ShapeDtypeStruct((tokens, kv_heads * width), jnp.bfloat16)] * 2,
        name="attend",
    )(table, queries, sibling_queries, *pieces)


def shards(queries, keys, values, vertical_blocks, vertical_count, slash_offsets, slash_count):
    tokens = queries.shape[0]
    ranks = lax.axis_size("seq")
    cores = lax.axis_size("tp")
    assert tokens == MASK_BLOCK_SIZE and cores == 2
    rank = lax.axis_index("seq")
    core = lax.axis_index("tp")
    columns = 2
    relay = ranks == 8
    lines = ranks // columns
    half = KEY_VALUE_HEADS // cores
    swap = [(0, 1), (1, 0)]

    parts = [vertical_blocks, vertical_count, slash_offsets, slash_count, rank, core]
    sizes = [part.size for part in parts]
    offsets = tuple(sum(sizes[:n]) for n in range(len(sizes)))
    table = jnp.concatenate([part.astype(jnp.int32).reshape(-1) for part in parts])
    common = (vertical_blocks.shape[1], slash_offsets.shape[1], offsets)

    def by_head(array):
        return array.reshape(tokens, cores, half, HEAD_SIZE).transpose(1, 2, 0, 3)

    stacked = jnp.stack([by_head(keys), by_head(values)], axis=2)
    own = lax.dynamic_index_in_dim(stacked, core, 0, False)
    other = lax.dynamic_index_in_dim(stacked, cores - 1 - core, 0, False)
    other = lax.ppermute(other, "tp", swap)
    local = jnp.concatenate([own, other], axis=2)[None]
    query_width = QUERY_HEADS // cores * HEAD_SIZE
    sibling_queries = lax.ppermute(
        lax.dynamic_slice_in_dim(queries, (cores - 1 - core) * query_width, query_width, 1), "tp", swap
    )

    if not relay:
        gathered = lax.all_gather(local[0], "seq", axis=0)
        geometry = (False, columns, cores, 0) + common + (((ranks, tuple(range(ranks))),),)
        own_out, sibling_out = attend(table, geometry, queries, sibling_queries, [gathered], half)
        sibling_out = lax.ppermute(sibling_out, "tp", swap)
    else:
        first = half - 1

        def along(array, step):
            pairs = [
                (line * columns + column, (line + 1) * columns + column)
                for line in range(step - 1, lines - 1)
                for column in range(columns)
            ]
            return lax.ppermute(array, "seq", pairs)

        def across(array, step):
            pairs = [
                (line * columns + column, line * columns + 1 - column)
                for line in range(step, lines)
                for column in range(columns)
            ]
            return lax.ppermute(array, "seq", pairs)

        a = [local[:, :first]]
        b_own = local[:, first:]
        b = [jnp.concatenate([b_own, across(b_own, 0)], axis=0)]
        for step in range(1, lines):
            a.append(along(a[-1], step))
        across_a = [across(a[step], step) for step in range(lines)]
        for step in range(1, lines):
            b.append(along(b[-1], step))
        layout_a = tuple((1, (step * columns,)) for step in range(lines)) + tuple(
            (1, (step * columns + 1,)) for step in range(lines)
        )
        layout_b = tuple((columns, (step * columns, step * columns + 1)) for step in range(lines))
        own_a, sibling_a = attend(
            table, (True, columns, cores, 0) + common + (layout_a,), queries, sibling_queries, a + across_a, first
        )
        sibling_a = lax.ppermute(sibling_a, "tp", swap)
        own_b, sibling_b = attend(
            table, (True, columns, cores, first) + common + (layout_b,), queries, sibling_queries, b, half - first
        )
        sibling_b = lax.ppermute(sibling_b, "tp", swap)
        own_out = jnp.concatenate([own_a, own_b], axis=1)
        sibling_out = jnp.concatenate([sibling_a, sibling_b], axis=1)
    low = jnp.where(core == 0, own_out, sibling_out)
    high = jnp.where(core == 0, sibling_out, own_out)
    return jnp.concatenate([low, high], axis=1)


def solution(mesh):
    return jax.shard_map(
        shards,
        mesh=mesh,
        in_specs=(
            P(("groups", "seq", "tp"), None),
            P(("groups", "seq", "tp"), None),
            P(("groups", "seq", "tp"), None),
            P(),
            P(),
            P(),
            P(),
        ),
        out_specs=P(("groups", "seq", "tp"), None),
        check_vma=False,
    )
```

```python
import functools

import jax
import jax.numpy as jnp
from jax import lax
from jax.experimental import pallas as pl
from jax.experimental.pallas import tpu as pltpu
from jax.sharding import PartitionSpec as P

QUERY_HEADS = 64
KEY_VALUE_HEADS = 8
HEAD_SIZE = 128
MASK_BLOCK_SIZE = 128
GROUP = QUERY_HEADS // KEY_VALUE_HEADS
LOG2E = 1.4426950408889634


def attend_kernel(plan, table, *refs):
    relay, columns, cores, kv_first, kv_heads, own, sibling, slots, copies, offsets, widths, aliased = plan
    refs = list(refs)
    own_queries = refs.pop(0) if own else None
    sibling_queries = refs.pop(0) if sibling else None
    pieces = [refs.pop(0) for _ in slots]
    copied = [refs.pop(0) for _ in copies]
    if aliased:
        refs.pop(0)
    out = refs.pop(0) if own else None
    sibling_out = refs.pop(0) if sibling else None
    rows_held, own_held, own_made, sibling_held, sibling_made, sems, out_sems = refs
    vertical_at, vertical_count_at, slash_at, slash_count_at, rank_at, core_at = offsets
    vertical_width, slash_width = widths
    chip_rows = cores * MASK_BLOCK_SIZE
    width = GROUP * HEAD_SIZE
    half = KEY_VALUE_HEADS // cores
    rank = table[rank_at]
    core = table[core_at]
    other = cores - 1 - core

    moves = []
    for at, (piece, slot) in enumerate(zip(pieces, slots)):
        held = rows_held.at[pl.ds(slot * chip_rows, piece.shape[0])]
        moves.append(pltpu.make_async_copy(piece, held, sems.at[at]))
    if own:
        lanes = pl.ds(pl.multiple_of((core * half + kv_first) * width, width), kv_heads * width)
        moves.append(pltpu.make_async_copy(own_queries.at[:, lanes], own_held, sems.at[len(slots)]))
    if sibling:
        lanes = pl.ds(kv_first * width, kv_heads * width)
        moves.append(pltpu.make_async_copy(sibling_queries.at[:, lanes], sibling_held, sems.at[len(slots) + 1]))
    for move in moves:
        move.start()
    placed = []
    for at, (ref, first) in enumerate(zip(copied, copies)):
        lanes = pl.ds(pl.multiple_of((other * half + first) * width, width), ref.shape[1])
        placed.append(pltpu.make_async_copy(ref, out.at[:, lanes], sems.at[len(slots) + 2 + at]))
    for move in placed:
        move.start()
    for move in moves:
        move.wait()

    square = (MASK_BLOCK_SIZE, MASK_BLOCK_SIZE)
    causal = lax.broadcasted_iota(jnp.int32, square, 0) >= lax.broadcasted_iota(jnp.int32, square, 1)
    ones = jnp.ones(square, jnp.bfloat16)
    factor = HEAD_SIZE**-0.5 * LOG2E
    own_row = (0 if relay else rank) * chip_rows

    def row_of(block):
        chip = block // cores
        if relay:
            slot = (rank // columns - chip // columns) * columns + jnp.bitwise_xor(rank % columns, chip % columns)
        else:
            slot = chip
        return (slot * cores + jnp.bitwise_xor(block % cores, core)) * MASK_BLOCK_SIZE

    def unit(queries, block, diagonal_row, head, kv):
        rows = [diagonal_row]
        active = [None]
        verticals = []
        for entry in range(vertical_width):
            vertical = table[vertical_at + head * vertical_width + entry]
            live = entry < table[vertical_count_at + head]
            verticals.append((vertical, live))
            use = live & (vertical < block)
            rows.append(row_of(jnp.where(use, vertical, block)))
            active.append(use)
        for entry in range(slash_width):
            target = block - table[slash_at + head * slash_width + entry]
            use = (entry < table[slash_count_at + head]) & (target >= 0)
            for vertical, live in verticals:
                use = use & jnp.logical_not(live & (vertical == target))
            rows.append(row_of(jnp.where(use, target, block)))
            active.append(use)
        rows = [pl.ds(pl.multiple_of(row, MASK_BLOCK_SIZE), MASK_BLOCK_SIZE) for row in rows]
        key_lanes = pl.ds(pl.multiple_of(kv * HEAD_SIZE, HEAD_SIZE), HEAD_SIZE)
        value_lanes = pl.ds(pl.multiple_of((kv_heads + kv) * HEAD_SIZE, HEAD_SIZE), HEAD_SIZE)
        keys = jnp.concatenate([rows_held[row, key_lanes] for row in rows], axis=0)
        values = jnp.concatenate(
            [jnp.concatenate([rows_held[row, value_lanes], ones], axis=1) for row in rows], axis=0
        )
        scores = lax.dot_general(queries, keys, (((1,), (1,)), ((), ())), preferred_element_type=jnp.float32)
        tiles = []
        for index, use in enumerate(active):
            tile = scores[:, index * MASK_BLOCK_SIZE : (index + 1) * MASK_BLOCK_SIZE]
            tiles.append(jnp.where(causal if use is None else use, tile, -jnp.inf))
        peak = functools.reduce(jnp.maximum, tiles)
        peak = jnp.max(peak, axis=1, keepdims=True)
        weights = [jnp.exp2((tile - peak) * factor).astype(jnp.bfloat16) for tile in tiles]
        sums = jnp.dot(jnp.concatenate(weights, axis=1), values, preferred_element_type=jnp.float32)
        return (sums[:, :HEAD_SIZE] / sums[:, HEAD_SIZE:]).astype(jnp.bfloat16)

    def results(kv):
        lanes = pl.ds(pl.multiple_of(kv * width, width), width)
        made = []
        if own:
            target = pl.ds(pl.multiple_of((core * half + kv_first + kv) * width, width), width)
            made.append(pltpu.make_async_copy(own_made.at[:, lanes], out.at[:, target], out_sems.at[kv, 0]))
        if sibling:
            made.append(pltpu.make_async_copy(sibling_made.at[:, lanes], sibling_out.at[:, lanes], out_sems.at[kv, 1]))
        return made

    def of_head(kv, carry):
        for slot in range(GROUP):
            head = (core * half + kv_first + kv) * GROUP + slot
            lanes = pl.ds(pl.multiple_of(kv * width + slot * HEAD_SIZE, HEAD_SIZE), HEAD_SIZE)
            if own:
                own_made[:, lanes] = unit(own_held[:, lanes], rank * cores + core, own_row, head, kv)
            if sibling:
                sibling_made[:, lanes] = unit(
                    sibling_held[:, lanes], rank * cores + other, own_row + MASK_BLOCK_SIZE, head, kv
                )
        for move in results(kv):
            move.start()
        return carry

    lax.fori_loop(0, kv_heads, of_head, 0)
    for kv in range(kv_heads):
        for move in results(kv):
            move.wait()
    for move in placed:
        move.wait()


def attend(table, common, kv_first, kv_heads, queries, sibling_queries, pieces, slots, copies=(), into=None):
    relay, columns, cores, offsets, widths = common
    own, sibling = queries is not None, sibling_queries is not None
    some = queries if own else sibling_queries
    tokens = some.shape[0]
    width = kv_heads * GROUP * HEAD_SIZE
    plan = (relay, columns, cores, kv_first, kv_heads, own, sibling, tuple(slots), tuple(first for _, first in copies))
    plan += (offsets, widths, into is not None)
    operands = [array for array in (queries, sibling_queries) if array is not None]
    operands += list(pieces) + [array for array, _ in copies]
    aliases = {}
    if into is not None:
        aliases = {1 + len(operands): 0}
        operands.append(into)
    shapes = []
    if own:
        shapes.append(jax.ShapeDtypeStruct((tokens, QUERY_HEADS * HEAD_SIZE), jnp.bfloat16))
    if sibling:
        shapes.append(jax.ShapeDtypeStruct((tokens, width), jnp.bfloat16))
    anywhere = pl.BlockSpec(memory_space=pl.ANY)
    held = pltpu.VMEM((tokens, width), jnp.bfloat16)
    small = pltpu.VMEM((16, HEAD_SIZE), jnp.bfloat16)
    rows = sum(piece.shape[0] for piece in pieces)
    return pl.pallas_call(
        functools.partial(attend_kernel, plan),
        grid_spec=pltpu.PrefetchScalarGridSpec(
            num_scalar_prefetch=1,
            grid=(),
            in_specs=[anywhere] * len(operands),
            out_specs=[anywhere] * len(shapes),
            scratch_shapes=[pltpu.VMEM((rows, 2 * kv_heads * HEAD_SIZE), jnp.bfloat16)]
            + [held if own else small] * 2
            + [held if sibling else small] * 2
            + [
                pltpu.SemaphoreType.DMA((len(pieces) + 2 + max(1, len(copies)),)),
                pltpu.SemaphoreType.DMA((kv_heads, 2)),
            ],
        ),
        out_shape=shapes,
        input_output_aliases=aliases,
        name="attend",
    )(table, *operands)


def shards(queries, keys, values, vertical_blocks, vertical_count, slash_offsets, slash_count):
    tokens = queries.shape[0]
    ranks = lax.axis_size("seq")
    cores = lax.axis_size("tp")
    assert tokens == MASK_BLOCK_SIZE and cores == 2
    rank = lax.axis_index("seq")
    core = lax.axis_index("tp")
    other = cores - 1 - core
    columns = 2
    relay = ranks == 8
    lines = ranks // columns
    half = KEY_VALUE_HEADS // cores
    group_width = GROUP * HEAD_SIZE
    swap = [(0, 1), (1, 0)]
    chunks = ((0, half // 2), (half // 2, half - half // 2))

    parts = [vertical_blocks, vertical_count, slash_offsets, slash_count, rank, core]
    sizes = [part.size for part in parts]
    offsets = tuple(sum(sizes[:n]) for n in range(len(sizes)))
    table = jnp.concatenate([part.astype(jnp.int32).reshape(-1) for part in parts])
    common = (relay, columns, cores, offsets, (vertical_blocks.shape[1], slash_offsets.shape[1]))

    def taken(of_core, first, count):
        start = (of_core * half + first) * HEAD_SIZE
        return jnp.concatenate(
            [lax.dynamic_slice_in_dim(array, start, count * HEAD_SIZE, 1) for array in (keys, values)], axis=1
        )

    local = []
    for (first, count) in chunks:
        got = lax.ppermute(taken(other, first, count), "tp", swap)
        local.append(jnp.concatenate([taken(core, first, count), got], axis=0))
    sibling_queries = lax.ppermute(
        lax.dynamic_slice_in_dim(queries, other * half * group_width, half * group_width, 1), "tp", swap
    )

    if relay:

        def along(array, step):
            pairs = [
                (line * columns + column, (line + 1) * columns + column)
                for line in range(step - 1, lines - 1)
                for column in range(columns)
            ]
            return lax.ppermute(array, "seq", pairs)

        def across(array, step):
            pairs = [
                (line * columns + column, line * columns + 1 - column)
                for line in range(step, lines)
                for column in range(columns)
            ]
            return lax.ppermute(array, "seq", pairs)

        gathered = []
        for name, piece in zip("ab", local):
            line_pieces = [piece]
            for step in range(1, lines):
                line_pieces.append(along(line_pieces[-1], step))
            last = lines if name == "a" else lines - 1
            cross_pieces = [across(line_pieces[step], step) for step in range(last)]
            if name == "b":
                pairs = [(column, (lines - 1) * columns + column) for column in range(columns)]
                cross_pieces.append(lax.ppermute(cross_pieces[0], "seq", pairs))
            gathered.append(line_pieces + cross_pieces)
        slots = [step * columns for step in range(lines)] + [step * columns + 1 for step in range(lines)]
    else:
        gathered = [[lax.all_gather(piece, "seq", axis=0, tiled=True)] for piece in local]
        slots = [0]

    (first_a, count_a), (first_b, count_b) = chunks
    out, sibling_a = attend(table, common, first_a, count_a, queries, sibling_queries, gathered[0], slots)
    got_a = lax.ppermute(sibling_a, "tp", swap)
    (sibling_b,) = attend(table, common, first_b, count_b, None, sibling_queries, gathered[1], slots)
    got_b = lax.ppermute(sibling_b, "tp", swap)
    (out,) = attend(
        table, common, first_b, count_b, queries, None, gathered[1], slots, [(got_a, first_a)], out
    )
    return lax.dynamic_update_slice_in_dim(out, got_b, (other * half + first_b) * group_width, 1)


def solution(mesh):
    return jax.shard_map(
        shards,
        mesh=mesh,
        in_specs=(
            P(("groups", "seq", "tp"), None),
            P(("groups", "seq", "tp"), None),
            P(("groups", "seq", "tp"), None),
            P(),
            P(),
            P(),
            P(),
        ),
        out_specs=P(("groups", "seq", "tp"), None),
        check_vma=False,
    )
```

```python
import functools

import jax
import jax.numpy as jnp
from jax import lax
from jax.experimental import pallas as pl
from jax.experimental.pallas import tpu as pltpu
from jax.sharding import PartitionSpec as P

QUERY_HEADS = 64
KEY_VALUE_HEADS = 8
HEAD_SIZE = 128
MASK_BLOCK_SIZE = 128
GROUP = QUERY_HEADS // KEY_VALUE_HEADS
LOG2E = 1.4426950408889634


def attend_kernel(plan, table, *refs):
    relay, columns, cores, kv_first, kv_heads, own, sibling, slots, copies, offsets, widths, aliased = plan
    refs = list(refs)
    own_queries = refs.pop(0) if own else None
    sibling_queries = refs.pop(0) if sibling else None
    pieces = [refs.pop(0) for _ in slots]
    copied = [refs.pop(0) for _ in copies]
    if aliased:
        refs.pop(0)
    out = refs.pop(0) if own else None
    sibling_out = refs.pop(0) if sibling else None
    rows_held, own_held, own_made, sibling_held, sibling_made, sems, out_sems = refs
    vertical_at, vertical_count_at, slash_at, slash_count_at, rank_at, core_at = offsets
    vertical_width, slash_width = widths
    chip_rows = cores * MASK_BLOCK_SIZE
    width = GROUP * HEAD_SIZE
    half = KEY_VALUE_HEADS // cores
    rank = table[rank_at]
    core = table[core_at]
    other = cores - 1 - core

    moves = []
    for at, (piece, slot) in enumerate(zip(pieces, slots)):
        held = rows_held.at[pl.ds(slot * chip_rows, piece.shape[0])]
        moves.append(pltpu.make_async_copy(piece, held, sems.at[at]))
    if own:
        lanes = pl.ds(pl.multiple_of((core * half + kv_first) * width, width), kv_heads * width)
        moves.append(pltpu.make_async_copy(own_queries.at[:, lanes], own_held, sems.at[len(slots)]))
    if sibling:
        lanes = pl.ds(kv_first * width, kv_heads * width)
        moves.append(pltpu.make_async_copy(sibling_queries.at[:, lanes], sibling_held, sems.at[len(slots) + 1]))
    for move in moves:
        move.start()
    placed = []
    for at, (ref, first) in enumerate(zip(copied, copies)):
        lanes = pl.ds(pl.multiple_of((other * half + first) * width, width), ref.shape[1])
        placed.append(pltpu.make_async_copy(ref, out.at[:, lanes], sems.at[len(slots) + 2 + at]))
    for move in placed:
        move.start()
    for move in moves:
        move.wait()

    square = (MASK_BLOCK_SIZE, MASK_BLOCK_SIZE)
    causal = lax.broadcasted_iota(jnp.int32, square, 0) >= lax.broadcasted_iota(jnp.int32, square, 1)
    ones = jnp.ones(square, jnp.bfloat16)
    factor = HEAD_SIZE**-0.5 * LOG2E
    own_row = (0 if relay else rank) * chip_rows

    def row_of(block):
        chip = block // cores
        if relay:
            slot = (rank // columns - chip // columns) * columns + jnp.bitwise_xor(rank % columns, chip % columns)
        else:
            slot = chip
        return (slot * cores + jnp.bitwise_xor(block % cores, core)) * MASK_BLOCK_SIZE

    def unit(queries, block, diagonal_row, head, kv):
        rows = [diagonal_row]
        active = [None]
        verticals = []
        for entry in range(vertical_width):
            vertical = table[vertical_at + head * vertical_width + entry]
            live = entry < table[vertical_count_at + head]
            verticals.append((vertical, live))
            use = live & (vertical < block)
            rows.append(row_of(jnp.where(use, vertical, block)))
            active.append(use)
        for entry in range(slash_width):
            target = block - table[slash_at + head * slash_width + entry]
            use = (entry < table[slash_count_at + head]) & (target >= 0)
            for vertical, live in verticals:
                use = use & jnp.logical_not(live & (vertical == target))
            rows.append(row_of(jnp.where(use, target, block)))
            active.append(use)
        rows = [pl.ds(pl.multiple_of(row, MASK_BLOCK_SIZE), MASK_BLOCK_SIZE) for row in rows]
        key_lanes = pl.ds(pl.multiple_of(kv * HEAD_SIZE, HEAD_SIZE), HEAD_SIZE)
        value_lanes = pl.ds(pl.multiple_of((kv_heads + kv) * HEAD_SIZE, HEAD_SIZE), HEAD_SIZE)
        keys = jnp.concatenate([rows_held[row, key_lanes] for row in rows], axis=0)
        values = jnp.concatenate(
            [jnp.concatenate([rows_held[row, value_lanes], ones], axis=1) for row in rows], axis=0
        )
        scores = lax.dot_general(queries, keys, (((1,), (1,)), ((), ())), preferred_element_type=jnp.float32)
        tiles = []
        for index, use in enumerate(active):
            tile = scores[:, index * MASK_BLOCK_SIZE : (index + 1) * MASK_BLOCK_SIZE]
            tiles.append(jnp.where(causal if use is None else use, tile, -jnp.inf))
        peak = functools.reduce(jnp.maximum, tiles)
        peak = jnp.max(peak, axis=1, keepdims=True)
        weights = [jnp.exp2((tile - peak) * factor).astype(jnp.bfloat16) for tile in tiles]
        sums = jnp.dot(jnp.concatenate(weights, axis=1), values, preferred_element_type=jnp.float32)
        return (sums[:, :HEAD_SIZE] / sums[:, HEAD_SIZE:]).astype(jnp.bfloat16)

    def results(kv):
        lanes = pl.ds(pl.multiple_of(kv * width, width), width)
        made = []
        if own:
            target = pl.ds(pl.multiple_of((core * half + kv_first + kv) * width, width), width)
            made.append(pltpu.make_async_copy(own_made.at[:, lanes], out.at[:, target], out_sems.at[kv, 0]))
        if sibling:
            made.append(pltpu.make_async_copy(sibling_made.at[:, lanes], sibling_out.at[:, lanes], out_sems.at[kv, 1]))
        return made

    def of_head(kv, carry):
        for slot in range(GROUP):
            head = (core * half + kv_first + kv) * GROUP + slot
            lanes = pl.ds(pl.multiple_of(kv * width + slot * HEAD_SIZE, HEAD_SIZE), HEAD_SIZE)
            if own:
                own_made[:, lanes] = unit(own_held[:, lanes], rank * cores + core, own_row, head, kv)
            if sibling:
                sibling_made[:, lanes] = unit(
                    sibling_held[:, lanes], rank * cores + other, own_row + MASK_BLOCK_SIZE, head, kv
                )
        for move in results(kv):
            move.start()
        return carry

    lax.fori_loop(0, kv_heads, of_head, 0)
    for kv in range(kv_heads):
        for move in results(kv):
            move.wait()
    for move in placed:
        move.wait()


def attend(table, common, kv_first, kv_heads, queries, sibling_queries, pieces, slots, copies=(), into=None):
    relay, columns, cores, offsets, widths = common
    own, sibling = queries is not None, sibling_queries is not None
    some = queries if own else sibling_queries
    tokens = some.shape[0]
    width = kv_heads * GROUP * HEAD_SIZE
    plan = (relay, columns, cores, kv_first, kv_heads, own, sibling, tuple(slots), tuple(first for _, first in copies))
    plan += (offsets, widths, into is not None)
    operands = [array for array in (queries, sibling_queries) if array is not None]
    operands += list(pieces) + [array for array, _ in copies]
    aliases = {}
    if into is not None:
        aliases = {1 + len(operands): 0}
        operands.append(into)
    shapes = []
    if own:
        shapes.append(jax.ShapeDtypeStruct((tokens, QUERY_HEADS * HEAD_SIZE), jnp.bfloat16))
    if sibling:
        shapes.append(jax.ShapeDtypeStruct((tokens, width), jnp.bfloat16))
    anywhere = pl.BlockSpec(memory_space=pl.ANY)
    held = pltpu.VMEM((tokens, width), jnp.bfloat16)
    small = pltpu.VMEM((16, HEAD_SIZE), jnp.bfloat16)
    rows = sum(piece.shape[0] for piece in pieces)
    return pl.pallas_call(
        functools.partial(attend_kernel, plan),
        grid_spec=pltpu.PrefetchScalarGridSpec(
            num_scalar_prefetch=1,
            grid=(),
            in_specs=[anywhere] * len(operands),
            out_specs=[anywhere] * len(shapes),
            scratch_shapes=[pltpu.VMEM((rows, 2 * kv_heads * HEAD_SIZE), jnp.bfloat16)]
            + [held if own else small] * 2
            + [held if sibling else small] * 2
            + [
                pltpu.SemaphoreType.DMA((len(pieces) + 2 + max(1, len(copies)),)),
                pltpu.SemaphoreType.DMA((kv_heads, 2)),
            ],
        ),
        out_shape=shapes,
        input_output_aliases=aliases,
        name="attend",
    )(table, *operands)


def shards(queries, keys, values, vertical_blocks, vertical_count, slash_offsets, slash_count):
    tokens = queries.shape[0]
    ranks = lax.axis_size("seq")
    cores = lax.axis_size("tp")
    assert tokens == MASK_BLOCK_SIZE and cores == 2
    rank = lax.axis_index("seq")
    core = lax.axis_index("tp")
    other = cores - 1 - core
    columns = 2
    relay = ranks == 8
    lines = ranks // columns
    half = KEY_VALUE_HEADS // cores
    group_width = GROUP * HEAD_SIZE
    swap = [(0, 1), (1, 0)]
    chunks = ((0, half // 2), (half // 2, half - half // 2))

    parts = [vertical_blocks, vertical_count, slash_offsets, slash_count, rank, core]
    sizes = [part.size for part in parts]
    offsets = tuple(sum(sizes[:n]) for n in range(len(sizes)))
    table = jnp.concatenate([part.astype(jnp.int32).reshape(-1) for part in parts])
    common = (relay, columns, cores, offsets, (vertical_blocks.shape[1], slash_offsets.shape[1]))

    def taken(of_core, first, count):
        start = (of_core * half + first) * HEAD_SIZE
        return jnp.concatenate(
            [lax.dynamic_slice_in_dim(array, start, count * HEAD_SIZE, 1) for array in (keys, values)], axis=1
        )

    local = []
    for (first, count) in chunks:
        got = lax.ppermute(taken(other, first, count), "tp", swap)
        local.append(jnp.concatenate([taken(core, first, count), got], axis=0))
    sibling_queries = lax.ppermute(
        lax.dynamic_slice_in_dim(queries, other * half * group_width, half * group_width, 1), "tp", swap
    )

    if relay:

        def along(array, step):
            pairs = [
                (line * columns + column, (line + 1) * columns + column)
                for line in range(step - 1, lines - 1)
                for column in range(columns)
            ]
            return lax.ppermute(array, "seq", pairs)

        def across(array, step):
            pairs = [
                (line * columns + column, line * columns + 1 - column)
                for line in range(step, lines)
                for column in range(columns)
            ]
            return lax.ppermute(array, "seq", pairs)

        gathered = []
        for name, piece in zip("ab", local):
            line_pieces = [piece]
            for step in range(1, lines):
                line_pieces.append(along(line_pieces[-1], step))
            last = lines if name == "a" else lines - 1
            cross_pieces = [across(line_pieces[step], step) for step in range(last)]
            if name == "b":
                pairs = [(column, (lines - 1) * columns + column) for column in range(columns)]
                cross_pieces.append(lax.ppermute(cross_pieces[0], "seq", pairs))
            gathered.append(line_pieces + cross_pieces)
        slots = [step * columns for step in range(lines)] + [step * columns + 1 for step in range(lines)]
    else:
        gathered = [[lax.all_gather(piece, "seq", axis=0, tiled=True)] for piece in local]
        slots = [0]

    (first_a, count_a), (first_b, count_b) = chunks
    out, sibling_a = attend(table, common, first_a, count_a, queries, sibling_queries, gathered[0], slots)
    got_a = lax.ppermute(sibling_a, "tp", swap)
    out, sibling_b = attend(
        table, common, first_b, count_b, queries, sibling_queries, gathered[1], slots, into=out
    )
    got_b = lax.ppermute(sibling_b, "tp", swap)
    for got, first in ((got_a, first_a), (got_b, first_b)):
        out = lax.dynamic_update_slice_in_dim(out, got, (other * half + first) * group_width, 1)
    return out


def solution(mesh):
    return jax.shard_map(
        shards,
        mesh=mesh,
        in_specs=(
            P(("groups", "seq", "tp"), None),
            P(("groups", "seq", "tp"), None),
            P(("groups", "seq", "tp"), None),
            P(),
            P(),
            P(),
            P(),
        ),
        out_specs=P(("groups", "seq", "tp"), None),
        check_vma=False,
    )
```

```python
import functools

import jax
import jax.numpy as jnp
from jax import lax
from jax.experimental import pallas as pl
from jax.experimental.pallas import tpu as pltpu
from jax.sharding import PartitionSpec as P

QUERY_HEADS = 64
KEY_VALUE_HEADS = 8
HEAD_SIZE = 128
MASK_BLOCK_SIZE = 128
GROUP = QUERY_HEADS // KEY_VALUE_HEADS
LOG2E = 1.4426950408889634


def attend_kernel(plan, table, *refs):
    relay, columns, cores, kv_first, kv_heads, own, sibling, slots, offsets, widths, aliased = plan
    refs = list(refs)
    own_queries = refs.pop(0) if own else None
    sibling_queries = refs.pop(0) if sibling else None
    pieces = [refs.pop(0) for _ in slots]
    if aliased:
        refs.pop(0)
    out = refs.pop(0) if own else None
    sibling_out = refs.pop(0) if sibling else None
    rows_held, own_held, own_made, sibling_held, sibling_made, sems, out_sems = refs
    vertical_at, vertical_count_at, slash_at, slash_count_at, rank_at, core_at = offsets
    vertical_width, slash_width = widths
    chip_rows = cores * MASK_BLOCK_SIZE
    width = GROUP * HEAD_SIZE
    half = KEY_VALUE_HEADS // cores
    rank = table[rank_at]
    core = table[core_at]
    other = cores - 1 - core

    moves = []
    for at, (piece, slot) in enumerate(zip(pieces, slots)):
        held = rows_held.at[pl.ds(slot * chip_rows, piece.shape[0])]
        moves.append(pltpu.make_async_copy(piece, held, sems.at[at]))
    if own:
        lanes = pl.ds(pl.multiple_of((core * half + kv_first) * width, width), kv_heads * width)
        moves.append(pltpu.make_async_copy(own_queries.at[:, lanes], own_held, sems.at[len(slots)]))
    if sibling:
        lanes = pl.ds(kv_first * width, kv_heads * width)
        moves.append(pltpu.make_async_copy(sibling_queries.at[:, lanes], sibling_held, sems.at[len(slots) + 1]))
    for move in moves:
        move.start()
    for move in moves:
        move.wait()

    square = (MASK_BLOCK_SIZE, MASK_BLOCK_SIZE)
    causal = lax.broadcasted_iota(jnp.int32, square, 0) >= lax.broadcasted_iota(jnp.int32, square, 1)
    ones = jnp.ones(square, jnp.bfloat16)
    factor = HEAD_SIZE**-0.5 * LOG2E
    own_row = (0 if relay else rank) * chip_rows

    def row_of(block):
        chip = block // cores
        if relay:
            slot = (rank // columns - chip // columns) * columns + jnp.bitwise_xor(rank % columns, chip % columns)
        else:
            slot = chip
        return (slot * cores + jnp.bitwise_xor(block % cores, core)) * MASK_BLOCK_SIZE

    def tile_rows(row):
        return pl.ds(pl.multiple_of(row, MASK_BLOCK_SIZE), MASK_BLOCK_SIZE)

    def product(left, rights):
        return lax.dot_general(
            left, jnp.concatenate(rights, axis=0), (((1,), (1,)), ((), ())), preferred_element_type=jnp.float32
        )

    def weighted(weights, rights):
        right = jnp.concatenate([jnp.concatenate([value, ones], axis=1) for value in rights], axis=0)
        return jnp.dot(weights, right, preferred_element_type=jnp.float32)

    def part(array, index, axis):
        return lax.slice_in_dim(array, index * MASK_BLOCK_SIZE, (index + 1) * MASK_BLOCK_SIZE, axis=axis)

    def results(kv):
        lanes = pl.ds(pl.multiple_of(kv * width, width), width)
        made = []
        if own:
            target = pl.ds(pl.multiple_of((core * half + kv_first + kv) * width, width), width)
            made.append(pltpu.make_async_copy(own_made.at[:, lanes], out.at[:, target], out_sems.at[kv, 0]))
        if sibling:
            made.append(pltpu.make_async_copy(sibling_made.at[:, lanes], sibling_out.at[:, lanes], out_sems.at[kv, 1]))
        return made

    def of_head(kv, carry):
        key_lanes = pl.ds(pl.multiple_of(kv * HEAD_SIZE, HEAD_SIZE), HEAD_SIZE)
        value_lanes = pl.ds(pl.multiple_of((kv_heads + kv) * HEAD_SIZE, HEAD_SIZE), HEAD_SIZE)
        sides = []
        if own:
            sides.append((own_held, own_made, rank * cores + core, own_row))
        if sibling:
            sides.append((sibling_held, sibling_made, rank * cores + other, own_row + MASK_BLOCK_SIZE))

        def lanes_of(slot):
            return pl.ds(pl.multiple_of(kv * width + slot * HEAD_SIZE, HEAD_SIZE), HEAD_SIZE)

        def key(row):
            return rows_held[tile_rows(row), key_lanes]

        def value(row):
            return rows_held[tile_rows(row), value_lanes]

        diagonal = [
            product(jnp.concatenate([held[:, lanes_of(slot)] for slot in range(GROUP)], axis=0), [key(row)])
            for held, _, _, row in sides
        ]
        pending = []
        for slot in range(GROUP):
            head = (core * half + kv_first + kv) * GROUP + slot
            queries = [held[:, lanes_of(slot)] for held, _, _, _ in sides]
            verticals = []
            for entry in range(vertical_width):
                vertical = table[vertical_at + head * vertical_width + entry]
                live = entry < table[vertical_count_at + head]
                verticals.append((vertical, live, row_of(jnp.minimum(vertical, rank * cores))))
            vertical_scores = product(jnp.concatenate(queries, axis=0), [key(row) for _, _, row in verticals])
            made = []
            for side, (_, _, block, diagonal_row) in enumerate(sides):
                slashes = []
                for entry in range(slash_width):
                    target = block - table[slash_at + head * slash_width + entry]
                    use = (entry < table[slash_count_at + head]) & (target >= 0)
                    for vertical, live, _ in verticals:
                        use = use & jnp.logical_not(live & (vertical == target))
                    slashes.append((use, row_of(jnp.where(use, target, block))))
                slash_scores = product(queries[side], [key(row) for _, row in slashes])
                tiles = [jnp.where(causal, part(diagonal[side], slot, 0), -jnp.inf)]
                across = part(vertical_scores, side, 0)
                for index, (vertical, live, _) in enumerate(verticals):
                    tiles.append(jnp.where(live & (vertical < block), part(across, index, 1), -jnp.inf))
                for index, (use, _) in enumerate(slashes):
                    tiles.append(jnp.where(use, part(slash_scores, index, 1), -jnp.inf))
                peak = jnp.max(functools.reduce(jnp.maximum, tiles), axis=1, keepdims=True)
                weights = [jnp.exp2((tile - peak) * factor).astype(jnp.bfloat16) for tile in tiles]
                last = 1 + len(verticals)
                total = weighted(jnp.concatenate(weights[last:], axis=1), [value(row) for _, row in slashes])
                made.append((weights[0], jnp.concatenate(weights[1:last], axis=1), total))
            vertical_sums = weighted(
                jnp.concatenate([one[1] for one in made], axis=0), [value(row) for _, _, row in verticals]
            )
            pending.append([(one[0], one[2] + part(vertical_sums, side, 0)) for side, one in enumerate(made)])
        for side, (_, to, _, diagonal_row) in enumerate(sides):
            sums = weighted(jnp.concatenate([one[side][0] for one in pending], axis=0), [value(diagonal_row)])
            for slot in range(GROUP):
                whole = part(sums, slot, 0) + pending[slot][side][1]
                to[:, lanes_of(slot)] = (whole[:, :HEAD_SIZE] / whole[:, HEAD_SIZE:]).astype(jnp.bfloat16)
            results(kv)[side].start()
        return carry

    lax.fori_loop(0, kv_heads, of_head, 0)
    for kv in range(kv_heads):
        for move in results(kv):
            move.wait()


def attend(table, common, kv_first, kv_heads, queries, sibling_queries, pieces, slots, into=None):
    relay, columns, cores, offsets, widths = common
    own, sibling = queries is not None, sibling_queries is not None
    some = queries if own else sibling_queries
    tokens = some.shape[0]
    width = kv_heads * GROUP * HEAD_SIZE
    plan = (relay, columns, cores, kv_first, kv_heads, own, sibling, tuple(slots), offsets, widths, into is not None)
    operands = [array for array in (queries, sibling_queries) if array is not None]
    operands += list(pieces)
    aliases = {}
    if into is not None:
        aliases = {1 + len(operands): 0}
        operands.append(into)
    shapes = []
    if own:
        shapes.append(jax.ShapeDtypeStruct((tokens, QUERY_HEADS * HEAD_SIZE), jnp.bfloat16))
    if sibling:
        shapes.append(jax.ShapeDtypeStruct((tokens, width), jnp.bfloat16))
    anywhere = pl.BlockSpec(memory_space=pl.ANY)
    held = pltpu.VMEM((tokens, width), jnp.bfloat16)
    small = pltpu.VMEM((16, HEAD_SIZE), jnp.bfloat16)
    rows = sum(piece.shape[0] for piece in pieces)
    return pl.pallas_call(
        functools.partial(attend_kernel, plan),
        grid_spec=pltpu.PrefetchScalarGridSpec(
            num_scalar_prefetch=1,
            grid=(),
            in_specs=[anywhere] * len(operands),
            out_specs=[anywhere] * len(shapes),
            scratch_shapes=[pltpu.VMEM((rows, 2 * kv_heads * HEAD_SIZE), jnp.bfloat16)]
            + [held if own else small] * 2
            + [held if sibling else small] * 2
            + [
                pltpu.SemaphoreType.DMA((len(pieces) + 2,)),
                pltpu.SemaphoreType.DMA((kv_heads, 2)),
            ],
        ),
        out_shape=shapes,
        input_output_aliases=aliases,
        name="attend",
    )(table, *operands)


def shards(queries, keys, values, vertical_blocks, vertical_count, slash_offsets, slash_count):
    tokens = queries.shape[0]
    ranks = lax.axis_size("seq")
    cores = lax.axis_size("tp")
    assert tokens == MASK_BLOCK_SIZE and cores == 2
    rank = lax.axis_index("seq")
    core = lax.axis_index("tp")
    other = cores - 1 - core
    columns = 2
    relay = ranks == 8
    lines = ranks // columns
    half = KEY_VALUE_HEADS // cores
    group_width = GROUP * HEAD_SIZE
    swap = [(0, 1), (1, 0)]
    chunks = ((0, half // 2), (half // 2, half - half // 2))

    parts = [vertical_blocks, vertical_count, slash_offsets, slash_count, rank, core]
    sizes = [part.size for part in parts]
    offsets = tuple(sum(sizes[:n]) for n in range(len(sizes)))
    table = jnp.concatenate([part.astype(jnp.int32).reshape(-1) for part in parts])
    common = (relay, columns, cores, offsets, (vertical_blocks.shape[1], slash_offsets.shape[1]))

    def taken(of_core, first, count):
        start = (of_core * half + first) * HEAD_SIZE
        return jnp.concatenate(
            [lax.dynamic_slice_in_dim(array, start, count * HEAD_SIZE, 1) for array in (keys, values)], axis=1
        )

    local = []
    for (first, count) in chunks:
        if local:
            keys, values, _ = lax.optimization_barrier((keys, values, local[0]))
        got = lax.ppermute(taken(other, first, count), "tp", swap)
        local.append(jnp.concatenate([taken(core, first, count), got], axis=0))
    sibling_queries = lax.ppermute(
        lax.dynamic_slice_in_dim(queries, other * half * group_width, half * group_width, 1), "tp", swap
    )

    if relay:

        def along(array, step):
            pairs = [
                (line * columns + column, (line + 1) * columns + column)
                for line in range(step - 1, lines - 1)
                for column in range(columns)
            ]
            return lax.ppermute(array, "seq", pairs)

        def across(array, step):
            pairs = [
                (line * columns + column, line * columns + 1 - column)
                for line in range(step, lines)
                for column in range(columns)
            ]
            return lax.ppermute(array, "seq", pairs)

        gathered = []
        for name, piece in zip("ab", local):
            line_pieces = [piece]
            for step in range(1, lines):
                line_pieces.append(along(line_pieces[-1], step))
            last = lines if name == "a" else lines - 1
            cross_pieces = [across(line_pieces[step], step) for step in range(last)]
            if name == "b":
                pairs = [(column, (lines - 1) * columns + column) for column in range(columns)]
                cross_pieces.append(lax.ppermute(cross_pieces[0], "seq", pairs))
            gathered.append(line_pieces + cross_pieces)
        slots = [step * columns for step in range(lines)] + [step * columns + 1 for step in range(lines)]
    else:
        gathered = [[lax.all_gather(piece, "seq", axis=0, tiled=True)] for piece in local]
        slots = [0]

    (first_a, count_a), (first_b, count_b) = chunks
    out, sibling_a = attend(table, common, first_a, count_a, queries, sibling_queries, gathered[0], slots)
    got_a = lax.ppermute(sibling_a, "tp", swap)
    out, sibling_b = attend(
        table, common, first_b, count_b, queries, sibling_queries, gathered[1], slots, into=out
    )
    got_b = lax.ppermute(sibling_b, "tp", swap)
    for got, first in ((got_a, first_a), (got_b, first_b)):
        out = lax.dynamic_update_slice_in_dim(out, got, (other * half + first) * group_width, 1)
    return out


def solution(mesh):
    return jax.shard_map(
        shards,
        mesh=mesh,
        in_specs=(
            P(("groups", "seq", "tp"), None),
            P(("groups", "seq", "tp"), None),
            P(("groups", "seq", "tp"), None),
            P(),
            P(),
            P(),
            P(),
        ),
        out_specs=P(("groups", "seq", "tp"), None),
        check_vma=False,
    )
```

```python
import functools

import jax
import jax.numpy as jnp
from jax import lax
from jax.experimental import pallas as pl
from jax.experimental.pallas import tpu as pltpu
from jax.sharding import PartitionSpec as P

QUERY_HEADS = 64
KEY_VALUE_HEADS = 8
HEAD_SIZE = 128
MASK_BLOCK_SIZE = 128
GROUP = QUERY_HEADS // KEY_VALUE_HEADS
LOG2E = 1.4426950408889634


def attend_kernel(plan, table, *refs):
    relay, columns, cores, kv_first, kv_heads, own, sibling, slots, offsets, widths, aliased = plan
    refs = list(refs)
    own_queries = refs.pop(0) if own else None
    sibling_queries = refs.pop(0) if sibling else None
    pieces = [refs.pop(0) for _ in slots]
    if aliased:
        refs.pop(0)
    out = refs.pop(0) if own else None
    sibling_out = refs.pop(0) if sibling else None
    rows_held, own_held, own_made, sibling_held, sibling_made, sems, out_sems = refs
    vertical_at, vertical_count_at, slash_at, slash_count_at, rank_at, core_at = offsets
    vertical_width, slash_width = widths
    chip_rows = cores * MASK_BLOCK_SIZE
    width = GROUP * HEAD_SIZE
    half = KEY_VALUE_HEADS // cores
    rank = table[rank_at]
    core = table[core_at]
    other = cores - 1 - core

    moves = []
    for at, (piece, slot) in enumerate(zip(pieces, slots)):
        held = rows_held.at[pl.ds(slot * chip_rows, piece.shape[0])]
        moves.append(pltpu.make_async_copy(piece, held, sems.at[at]))
    if own:
        lanes = pl.ds(pl.multiple_of((core * half + kv_first) * width, width), kv_heads * width)
        moves.append(pltpu.make_async_copy(own_queries.at[:, lanes], own_held, sems.at[len(slots)]))
    if sibling:
        lanes = pl.ds(kv_first * width, kv_heads * width)
        moves.append(pltpu.make_async_copy(sibling_queries.at[:, lanes], sibling_held, sems.at[len(slots) + 1]))
    for move in moves:
        move.start()
    for move in moves:
        move.wait()

    square = (MASK_BLOCK_SIZE, MASK_BLOCK_SIZE)
    causal = lax.broadcasted_iota(jnp.int32, square, 0) >= lax.broadcasted_iota(jnp.int32, square, 1)
    ones = jnp.ones(square, jnp.bfloat16)
    factor = HEAD_SIZE**-0.5 * LOG2E
    own_row = (0 if relay else rank) * chip_rows

    def row_of(block):
        chip = block // cores
        if relay:
            slot = (rank // columns - chip // columns) * columns + jnp.bitwise_xor(rank % columns, chip % columns)
        else:
            slot = chip
        return (slot * cores + jnp.bitwise_xor(block % cores, core)) * MASK_BLOCK_SIZE

    def tile_rows(row):
        return pl.ds(pl.multiple_of(row, MASK_BLOCK_SIZE), MASK_BLOCK_SIZE)

    def product(left, rights):
        return lax.dot_general(
            left, jnp.concatenate(rights, axis=0), (((1,), (1,)), ((), ())), preferred_element_type=jnp.float32
        )

    def weighted(weights, rights):
        right = jnp.concatenate([jnp.concatenate([value, ones], axis=1) for value in rights], axis=0)
        return jnp.dot(weights, right, preferred_element_type=jnp.float32)

    def part(array, index, axis):
        return lax.slice_in_dim(array, index * MASK_BLOCK_SIZE, (index + 1) * MASK_BLOCK_SIZE, axis=axis)

    def results(kv):
        lanes = pl.ds(pl.multiple_of(kv * width, width), width)
        made = []
        if own:
            target = pl.ds(pl.multiple_of((core * half + kv_first + kv) * width, width), width)
            made.append(pltpu.make_async_copy(own_made.at[:, lanes], out.at[:, target], out_sems.at[kv, 0]))
        if sibling:
            made.append(pltpu.make_async_copy(sibling_made.at[:, lanes], sibling_out.at[:, lanes], out_sems.at[kv, 1]))
        return made

    def of_head(kv, carry):
        key_lanes = pl.ds(pl.multiple_of(kv * HEAD_SIZE, HEAD_SIZE), HEAD_SIZE)
        value_lanes = pl.ds(pl.multiple_of((kv_heads + kv) * HEAD_SIZE, HEAD_SIZE), HEAD_SIZE)
        sides = []
        if own:
            sides.append((own_held, own_made, rank * cores + core, own_row))
        if sibling:
            sides.append((sibling_held, sibling_made, rank * cores + other, own_row + MASK_BLOCK_SIZE))

        def lanes_of(slot):
            return pl.ds(pl.multiple_of(kv * width + slot * HEAD_SIZE, HEAD_SIZE), HEAD_SIZE)

        def key(row):
            return rows_held[tile_rows(row), key_lanes]

        def value(row):
            return rows_held[tile_rows(row), value_lanes]

        diagonal = [
            product(jnp.concatenate([held[:, lanes_of(slot)] for slot in range(GROUP)], axis=0), [key(row)])
            for held, _, _, row in sides
        ]
        pending = []
        for slot in range(GROUP):
            head = (core * half + kv_first + kv) * GROUP + slot
            queries = [held[:, lanes_of(slot)] for held, _, _, _ in sides]
            verticals = []
            for entry in range(vertical_width):
                vertical = table[vertical_at + head * vertical_width + entry]
                live = entry < table[vertical_count_at + head]
                verticals.append((vertical, live, row_of(jnp.minimum(vertical, rank * cores))))
            vertical_scores = product(jnp.concatenate(queries, axis=0), [key(row) for _, _, row in verticals])
            made = []
            for side, (_, _, block, diagonal_row) in enumerate(sides):
                slashes = []
                for entry in range(slash_width):
                    target = block - table[slash_at + head * slash_width + entry]
                    use = (entry < table[slash_count_at + head]) & (target >= 0)
                    for vertical, live, _ in verticals:
                        use = use & jnp.logical_not(live & (vertical == target))
                    slashes.append((use, row_of(jnp.where(use, target, block))))
                slash_scores = product(queries[side], [key(row) for _, row in slashes])
                tiles = [jnp.where(causal, part(diagonal[side], slot, 0), -jnp.inf)]
                across = part(vertical_scores, side, 0)
                for index, (vertical, live, _) in enumerate(verticals):
                    tiles.append(jnp.where(live & (vertical < block), part(across, index, 1), -jnp.inf))
                for index, (use, _) in enumerate(slashes):
                    tiles.append(jnp.where(use, part(slash_scores, index, 1), -jnp.inf))
                peak = jnp.max(functools.reduce(jnp.maximum, tiles), axis=1, keepdims=True)
                weights = [jnp.exp2((tile - peak) * factor).astype(jnp.bfloat16) for tile in tiles]
                last = 1 + len(verticals)
                total = weighted(jnp.concatenate(weights[last:], axis=1), [value(row) for _, row in slashes])
                made.append((weights[0], jnp.concatenate(weights[1:last], axis=1), total))
            vertical_sums = weighted(
                jnp.concatenate([one[1] for one in made], axis=0), [value(row) for _, _, row in verticals]
            )
            pending.append([(one[0], one[2] + part(vertical_sums, side, 0)) for side, one in enumerate(made)])
        for side, (_, to, _, diagonal_row) in enumerate(sides):
            sums = weighted(jnp.concatenate([one[side][0] for one in pending], axis=0), [value(diagonal_row)])
            for slot in range(GROUP):
                whole = part(sums, slot, 0) + pending[slot][side][1]
                to[:, lanes_of(slot)] = (whole[:, :HEAD_SIZE] / whole[:, HEAD_SIZE:]).astype(jnp.bfloat16)
            results(kv)[side].start()
        return carry

    lax.fori_loop(0, kv_heads, of_head, 0)
    for kv in range(kv_heads):
        for move in results(kv):
            move.wait()


def attend(table, common, kv_first, kv_heads, queries, sibling_queries, pieces, slots, into=None):
    relay, columns, cores, offsets, widths = common
    own, sibling = queries is not None, sibling_queries is not None
    some = queries if own else sibling_queries
    tokens = some.shape[0]
    width = kv_heads * GROUP * HEAD_SIZE
    plan = (relay, columns, cores, kv_first, kv_heads, own, sibling, tuple(slots), offsets, widths, into is not None)
    operands = [array for array in (queries, sibling_queries) if array is not None]
    operands += list(pieces)
    aliases = {}
    if into is not None:
        aliases = {1 + len(operands): 0}
        operands.append(into)
    shapes = []
    if own:
        shapes.append(jax.ShapeDtypeStruct((tokens, QUERY_HEADS * HEAD_SIZE), jnp.bfloat16))
    if sibling:
        shapes.append(jax.ShapeDtypeStruct((tokens, width), jnp.bfloat16))
    anywhere = pl.BlockSpec(memory_space=pl.ANY)
    held = pltpu.VMEM((tokens, width), jnp.bfloat16)
    small = pltpu.VMEM((16, HEAD_SIZE), jnp.bfloat16)
    rows = sum(piece.shape[0] for piece in pieces)
    return pl.pallas_call(
        functools.partial(attend_kernel, plan),
        grid_spec=pltpu.PrefetchScalarGridSpec(
            num_scalar_prefetch=1,
            grid=(),
            in_specs=[anywhere] * len(operands),
            out_specs=[anywhere] * len(shapes),
            scratch_shapes=[pltpu.VMEM((rows, 2 * kv_heads * HEAD_SIZE), jnp.bfloat16)]
            + [held if own else small] * 2
            + [held if sibling else small] * 2
            + [
                pltpu.SemaphoreType.DMA((len(pieces) + 2,)),
                pltpu.SemaphoreType.DMA((kv_heads, 2)),
            ],
        ),
        out_shape=shapes,
        input_output_aliases=aliases,
        name="attend",
    )(table, *operands)


def shards(queries, keys, values, vertical_blocks, vertical_count, slash_offsets, slash_count):
    tokens = queries.shape[0]
    ranks = lax.axis_size("seq")
    cores = lax.axis_size("tp")
    assert tokens == MASK_BLOCK_SIZE and cores == 2
    rank = lax.axis_index("seq")
    core = lax.axis_index("tp")
    other = cores - 1 - core
    columns = 2
    lines = ranks // columns
    relay = lines == 4
    half = KEY_VALUE_HEADS // cores
    group_width = GROUP * HEAD_SIZE
    swap = [(0, 1), (1, 0)]
    chunks = ((0, half // 2), (half // 2, half - half // 2))

    parts = [vertical_blocks, vertical_count, slash_offsets, slash_count, rank, core]
    sizes = [part.size for part in parts]
    offsets = tuple(sum(sizes[:n]) for n in range(len(sizes)))
    table = jnp.concatenate([part.astype(jnp.int32).reshape(-1) for part in parts])
    common = (relay, columns, cores, offsets, (vertical_blocks.shape[1], slash_offsets.shape[1]))

    def taken(of_core, first, count):
        start = (of_core * half + first) * HEAD_SIZE
        return jnp.concatenate(
            [lax.dynamic_slice_in_dim(array, start, count * HEAD_SIZE, 1) for array in (keys, values)], axis=1
        )

    local = []
    for (first, count) in chunks:
        if local:
            keys, values, _ = lax.optimization_barrier((keys, values, local[0]))
        got = lax.ppermute(taken(other, first, count), "tp", swap)
        local.append(jnp.concatenate([taken(core, first, count), got], axis=0))
    sibling_queries = lax.ppermute(
        lax.dynamic_slice_in_dim(queries, other * half * group_width, half * group_width, 1), "tp", swap
    )

    if relay:

        def along(array, step):
            pairs = [
                (line * columns + column, (line + 1) * columns + column)
                for line in range(step - 1, lines - 1)
                for column in range(columns)
            ]
            return lax.ppermute(array, "seq", pairs)

        def across(array, step):
            pairs = [
                (line * columns + column, line * columns + 1 - column)
                for line in range(step, lines)
                for column in range(columns)
            ]
            return lax.ppermute(array, "seq", pairs)

        def from_first(array):
            pairs = [(column, (lines - 1) * columns + column) for column in range(columns)]
            return lax.ppermute(array, "seq", pairs)

        line_slots = [step * columns for step in range(lines)]
        a, b = [local[0]], [local[1]]
        a.append(along(a[0], 1))
        a.append(along(a[1], 2))
        a.append(from_first(a[0]))
        a += [across(a[step], step) for step in range(lines)]
        b.append(along(b[0], 1))
        b.append(along(b[1], 2))
        b += [across(b[step], step) for step in range(lines - 1)]
        both = jnp.concatenate([b[0], b[lines - 1]], axis=0)
        both, a[5], a[7], sibling_queries = lax.optimization_barrier((both, a[5], a[7], sibling_queries))
        b.append(from_first(both))
        gathered = [a, b]
        slots = [
            line_slots + [slot + 1 for slot in line_slots],
            line_slots[:-1] + [slot + 1 for slot in line_slots[:-1]] + line_slots[-1:],
        ]
    else:
        gathered = [[lax.all_gather(piece, "seq", axis=0, tiled=True)] for piece in local]
        slots = [[0], [0]]

    (first_a, count_a), (first_b, count_b) = chunks
    out, sibling_a = attend(table, common, first_a, count_a, queries, sibling_queries, gathered[0], slots[0])
    got_a = lax.ppermute(sibling_a, "tp", swap)
    out, sibling_b = attend(table, common, first_b, count_b, queries, sibling_queries, gathered[1], slots[1], into=out)
    got_b = lax.ppermute(sibling_b, "tp", swap)
    for got, first in ((got_a, first_a), (got_b, first_b)):
        out = lax.dynamic_update_slice_in_dim(out, got, (other * half + first) * group_width, 1)
    return out


def solution(mesh):
    return jax.shard_map(
        shards,
        mesh=mesh,
        in_specs=(
            P(("groups", "seq", "tp"), None),
            P(("groups", "seq", "tp"), None),
            P(("groups", "seq", "tp"), None),
            P(),
            P(),
            P(),
            P(),
        ),
        out_specs=P(("groups", "seq", "tp"), None),
        check_vma=False,
    )
```

```python
import functools

import jax
import jax.numpy as jnp
from jax import lax
from jax.experimental import pallas as pl
from jax.experimental.pallas import tpu as pltpu
from jax.sharding import PartitionSpec as P

QUERY_HEADS = 64
KEY_VALUE_HEADS = 8
HEAD_SIZE = 128
MASK_BLOCK_SIZE = 128
GROUP = QUERY_HEADS // KEY_VALUE_HEADS
LOG2E = 1.4426950408889634


def attend_kernel(plan, table, *refs):
    relay, columns, cores, kv_first, kv_heads, own, sibling, slots, offsets, widths, aliased = plan
    refs = list(refs)
    own_queries = refs.pop(0) if own else None
    sibling_queries = refs.pop(0) if sibling else None
    pieces = [refs.pop(0) for _ in slots]
    if aliased:
        refs.pop(0)
    out = refs.pop(0) if own else None
    sibling_out = refs.pop(0) if sibling else None
    rows_held, own_held, own_made, sibling_held, sibling_made, sems, out_sems = refs
    vertical_at, vertical_count_at, slash_at, slash_count_at, rank_at, core_at = offsets
    vertical_width, slash_width = widths
    chip_rows = cores * MASK_BLOCK_SIZE
    width = GROUP * HEAD_SIZE
    half = KEY_VALUE_HEADS // cores
    rank = table[rank_at]
    core = table[core_at]
    other = cores - 1 - core

    moves = []
    for at, (piece, slot) in enumerate(zip(pieces, slots)):
        held = rows_held.at[pl.ds(slot * chip_rows, piece.shape[0])]
        moves.append(pltpu.make_async_copy(piece, held, sems.at[at]))
    if own:
        lanes = pl.ds(pl.multiple_of((core * half + kv_first) * width, width), kv_heads * width)
        moves.append(pltpu.make_async_copy(own_queries.at[:, lanes], own_held, sems.at[len(slots)]))
    if sibling:
        lanes = pl.ds(kv_first * width, kv_heads * width)
        moves.append(pltpu.make_async_copy(sibling_queries.at[:, lanes], sibling_held, sems.at[len(slots) + 1]))
    for move in moves:
        move.start()
    for move in moves:
        move.wait()

    square = (MASK_BLOCK_SIZE, MASK_BLOCK_SIZE)
    causal = lax.broadcasted_iota(jnp.int32, square, 0) >= lax.broadcasted_iota(jnp.int32, square, 1)
    ones = jnp.ones(square, jnp.bfloat16)
    factor = HEAD_SIZE**-0.5 * LOG2E
    own_row = (0 if relay else rank) * chip_rows

    def row_of(block):
        chip = block // cores
        if relay:
            slot = (rank // columns - chip // columns) * columns + jnp.bitwise_xor(rank % columns, chip % columns)
        else:
            slot = chip
        return (slot * cores + jnp.bitwise_xor(block % cores, core)) * MASK_BLOCK_SIZE

    def tile_rows(row):
        return pl.ds(pl.multiple_of(row, MASK_BLOCK_SIZE), MASK_BLOCK_SIZE)

    def product(left, rights):
        return lax.dot_general(
            left, jnp.concatenate(rights, axis=0), (((1,), (1,)), ((), ())), preferred_element_type=jnp.float32
        )

    def weighted(weights, rights):
        right = jnp.concatenate([jnp.concatenate([value, ones], axis=1) for value in rights], axis=0)
        return jnp.dot(weights, right, preferred_element_type=jnp.float32)

    def part(array, index, axis):
        return lax.slice_in_dim(array, index * MASK_BLOCK_SIZE, (index + 1) * MASK_BLOCK_SIZE, axis=axis)

    def results(kv):
        lanes = pl.ds(pl.multiple_of(kv * width, width), width)
        made = []
        if own:
            target = pl.ds(pl.multiple_of((core * half + kv_first + kv) * width, width), width)
            made.append(pltpu.make_async_copy(own_made.at[:, lanes], out.at[:, target], out_sems.at[kv, 0]))
        if sibling:
            made.append(pltpu.make_async_copy(sibling_made.at[:, lanes], sibling_out.at[:, lanes], out_sems.at[kv, 1]))
        return made

    def of_head(kv, carry):
        key_lanes = pl.ds(pl.multiple_of(kv * HEAD_SIZE, HEAD_SIZE), HEAD_SIZE)
        value_lanes = pl.ds(pl.multiple_of((kv_heads + kv) * HEAD_SIZE, HEAD_SIZE), HEAD_SIZE)
        sides = []
        if own:
            sides.append((own_held, own_made, rank * cores + core, own_row))
        if sibling:
            sides.append((sibling_held, sibling_made, rank * cores + other, own_row + MASK_BLOCK_SIZE))

        def lanes_of(slot):
            return pl.ds(pl.multiple_of(kv * width + slot * HEAD_SIZE, HEAD_SIZE), HEAD_SIZE)

        def key(row):
            return rows_held[tile_rows(row), key_lanes]

        def value(row):
            return rows_held[tile_rows(row), value_lanes]

        diagonal = [
            product(jnp.concatenate([held[:, lanes_of(slot)] for slot in range(GROUP)], axis=0), [key(row)])
            for held, _, _, row in sides
        ]
        pending = []
        for slot in range(GROUP):
            head = (core * half + kv_first + kv) * GROUP + slot
            queries = [held[:, lanes_of(slot)] for held, _, _, _ in sides]
            verticals = []
            for entry in range(vertical_width):
                vertical = table[vertical_at + head * vertical_width + entry]
                live = entry < table[vertical_count_at + head]
                verticals.append((vertical, live, row_of(jnp.minimum(vertical, rank * cores))))
            vertical_scores = product(jnp.concatenate(queries, axis=0), [key(row) for _, _, row in verticals])
            made = []
            for side, (_, _, block, diagonal_row) in enumerate(sides):
                slashes = []
                for entry in range(slash_width):
                    target = block - table[slash_at + head * slash_width + entry]
                    use = (entry < table[slash_count_at + head]) & (target >= 0)
                    for vertical, live, _ in verticals:
                        use = use & jnp.logical_not(live & (vertical == target))
                    slashes.append((use, row_of(jnp.where(use, target, block))))
                slash_scores = product(queries[side], [key(row) for _, row in slashes])
                tiles = [jnp.where(causal, part(diagonal[side], slot, 0), -jnp.inf)]
                across = part(vertical_scores, side, 0)
                for index, (vertical, live, _) in enumerate(verticals):
                    tiles.append(jnp.where(live & (vertical < block), part(across, index, 1), -jnp.inf))
                for index, (use, _) in enumerate(slashes):
                    tiles.append(jnp.where(use, part(slash_scores, index, 1), -jnp.inf))
                peak = jnp.max(functools.reduce(jnp.maximum, tiles), axis=1, keepdims=True)
                weights = [jnp.exp2((tile - peak) * factor).astype(jnp.bfloat16) for tile in tiles]
                last = 1 + len(verticals)
                total = weighted(jnp.concatenate(weights[last:], axis=1), [value(row) for _, row in slashes])
                made.append((weights[0], jnp.concatenate(weights[1:last], axis=1), total))
            vertical_sums = weighted(
                jnp.concatenate([one[1] for one in made], axis=0), [value(row) for _, _, row in verticals]
            )
            pending.append([(one[0], one[2] + part(vertical_sums, side, 0)) for side, one in enumerate(made)])
        for side, (_, to, _, diagonal_row) in enumerate(sides):
            sums = weighted(jnp.concatenate([one[side][0] for one in pending], axis=0), [value(diagonal_row)])
            for slot in range(GROUP):
                whole = part(sums, slot, 0) + pending[slot][side][1]
                to[:, lanes_of(slot)] = (whole[:, :HEAD_SIZE] / whole[:, HEAD_SIZE:]).astype(jnp.bfloat16)
            results(kv)[side].start()
        return carry

    lax.fori_loop(0, kv_heads, of_head, 0)
    for kv in range(kv_heads):
        for move in results(kv):
            move.wait()


def attend(table, common, kv_first, kv_heads, queries, sibling_queries, pieces, slots, into=None):
    relay, columns, cores, offsets, widths = common
    own, sibling = queries is not None, sibling_queries is not None
    some = queries if own else sibling_queries
    tokens = some.shape[0]
    width = kv_heads * GROUP * HEAD_SIZE
    plan = (relay, columns, cores, kv_first, kv_heads, own, sibling, tuple(slots), offsets, widths, into is not None)
    operands = [array for array in (queries, sibling_queries) if array is not None]
    operands += list(pieces)
    aliases = {}
    if into is not None:
        aliases = {1 + len(operands): 0}
        operands.append(into)
    shapes = []
    if own:
        shapes.append(jax.ShapeDtypeStruct((tokens, QUERY_HEADS * HEAD_SIZE), jnp.bfloat16))
    if sibling:
        shapes.append(jax.ShapeDtypeStruct((tokens, width), jnp.bfloat16))
    anywhere = pl.BlockSpec(memory_space=pl.ANY)
    held = pltpu.VMEM((tokens, width), jnp.bfloat16)
    small = pltpu.VMEM((16, HEAD_SIZE), jnp.bfloat16)
    rows = sum(piece.shape[0] for piece in pieces)
    return pl.pallas_call(
        functools.partial(attend_kernel, plan),
        grid_spec=pltpu.PrefetchScalarGridSpec(
            num_scalar_prefetch=1,
            grid=(),
            in_specs=[anywhere] * len(operands),
            out_specs=[anywhere] * len(shapes),
            scratch_shapes=[pltpu.VMEM((rows, 2 * kv_heads * HEAD_SIZE), jnp.bfloat16)]
            + [held if own else small] * 2
            + [held if sibling else small] * 2
            + [
                pltpu.SemaphoreType.DMA((len(pieces) + 2,)),
                pltpu.SemaphoreType.DMA((kv_heads, 2)),
            ],
        ),
        out_shape=shapes,
        input_output_aliases=aliases,
        name="attend",
        compiler_params=pltpu.CompilerParams(vmem_limit_bytes=4 * rows * kv_heads * HEAD_SIZE + 2**23),
    )(table, *operands)


def shards(queries, keys, values, vertical_blocks, vertical_count, slash_offsets, slash_count):
    tokens = queries.shape[0]
    ranks = lax.axis_size("seq")
    cores = lax.axis_size("tp")
    assert tokens == MASK_BLOCK_SIZE and cores == 2
    rank = lax.axis_index("seq")
    core = lax.axis_index("tp")
    other = cores - 1 - core
    columns = 2
    lines = ranks // columns
    relay = lines == 4
    half = KEY_VALUE_HEADS // cores
    group_width = GROUP * HEAD_SIZE
    swap = [(0, 1), (1, 0)]
    chunks = ((0, half // 2), (half // 2, half - half // 2))

    parts = [vertical_blocks, vertical_count, slash_offsets, slash_count, rank, core]
    sizes = [part.size for part in parts]
    offsets = tuple(sum(sizes[:n]) for n in range(len(sizes)))
    table = jnp.concatenate([part.astype(jnp.int32).reshape(-1) for part in parts])
    common = (relay, columns, cores, offsets, (vertical_blocks.shape[1], slash_offsets.shape[1]))

    def taken(of_core, first, count):
        start = (of_core * half + first) * HEAD_SIZE
        return jnp.concatenate(
            [lax.dynamic_slice_in_dim(array, start, count * HEAD_SIZE, 1) for array in (keys, values)], axis=1
        )

    local = []
    for name, (first, count) in zip("ab", chunks):
        mine, theirs = taken(core, first, count), taken(other, first, count)
        if name == "b":
            mine, theirs = lax.optimization_barrier((mine, theirs))
        got = lax.ppermute(theirs, "tp", swap)
        local.append(jnp.concatenate([mine, got], axis=0))
    sibling_queries = lax.ppermute(
        lax.dynamic_slice_in_dim(queries, other * half * group_width, half * group_width, 1), "tp", swap
    )

    if relay:

        def along(array, step):
            pairs = [
                (line * columns + column, (line + 1) * columns + column)
                for line in range(step - 1, lines - 1)
                for column in range(columns)
            ]
            return lax.ppermute(array, "seq", pairs)

        def across(array, step):
            pairs = [
                (line * columns + column, line * columns + 1 - column)
                for line in range(step, lines)
                for column in range(columns)
            ]
            return lax.ppermute(array, "seq", pairs)

        def from_first(array):
            pairs = [(column, (lines - 1) * columns + column) for column in range(columns)]
            return lax.ppermute(array, "seq", pairs)

        line_slots = [step * columns for step in range(lines)]
        a, b = [local[0]], [local[1]]
        a.append(along(a[0], 1))
        a.append(along(a[1], 2))
        a.append(from_first(a[0]))
        a += [across(a[step], step) for step in range(lines)]
        b.append(along(b[0], 1))
        b.append(along(b[1], 2))
        b += [across(b[step], step) for step in range(lines - 1)]
        both = jnp.concatenate([b[0], b[lines - 1]], axis=0)
        b.append(from_first(both))
        gathered = [a, b]
        slots = [
            line_slots + [slot + 1 for slot in line_slots],
            line_slots[:-1] + [slot + 1 for slot in line_slots[:-1]] + line_slots[-1:],
        ]
    else:
        gathered = [[lax.all_gather(piece, "seq", axis=0, tiled=True)] for piece in local]
        slots = [[0], [0]]

    (first_a, count_a), (first_b, count_b) = chunks
    out, sibling_a = attend(table, common, first_a, count_a, queries, sibling_queries, gathered[0], slots[0])
    got_a = lax.ppermute(sibling_a, "tp", swap)
    out, sibling_b = attend(table, common, first_b, count_b, queries, sibling_queries, gathered[1], slots[1], into=out)
    got_b = lax.ppermute(sibling_b, "tp", swap)
    for got, first in ((got_a, first_a), (got_b, first_b)):
        out = lax.dynamic_update_slice_in_dim(out, got, (other * half + first) * group_width, 1)
    return out


def solution(mesh):
    return jax.shard_map(
        shards,
        mesh=mesh,
        in_specs=(
            P(("groups", "seq", "tp"), None),
            P(("groups", "seq", "tp"), None),
            P(("groups", "seq", "tp"), None),
            P(),
            P(),
            P(),
            P(),
        ),
        out_specs=P(("groups", "seq", "tp"), None),
        check_vma=False,
    )
```

```python
import functools

import jax
import jax.numpy as jnp
from jax import lax
from jax.experimental import pallas as pl
from jax.experimental.pallas import tpu as pltpu
from jax.sharding import PartitionSpec as P

QUERY_HEADS = 64
KEY_VALUE_HEADS = 8
HEAD_SIZE = 128
MASK_BLOCK_SIZE = 128
GROUP = QUERY_HEADS // KEY_VALUE_HEADS
LOG2E = 1.4426950408889634


def attend_kernel(plan, table, *refs):
    relay, columns, cores, kv_first, kv_heads, own, sibling, slots, offsets, widths, aliased = plan
    refs = list(refs)
    own_queries = refs.pop(0) if own else None
    sibling_queries = refs.pop(0) if sibling else None
    pieces = [refs.pop(0) for _ in slots]
    if aliased:
        refs.pop(0)
    out = refs.pop(0) if own else None
    sibling_out = refs.pop(0) if sibling else None
    rows_held, own_made, sibling_made, sems, out_sems = refs
    vertical_at, vertical_count_at, slash_at, slash_count_at, rank_at, core_at = offsets
    vertical_width, slash_width = widths
    chip_rows = cores * MASK_BLOCK_SIZE
    width = GROUP * HEAD_SIZE
    half = KEY_VALUE_HEADS // cores
    rank = table[rank_at]
    core = table[core_at]
    other = cores - 1 - core

    moves = []
    for at, (piece, slot) in enumerate(zip(pieces, slots)):
        held = rows_held.at[pl.ds(slot * chip_rows, piece.shape[0])]
        moves.append(pltpu.make_async_copy(piece, held, sems.at[at]))
    for move in moves:
        move.start()
    for move in moves:
        move.wait()

    square = (MASK_BLOCK_SIZE, MASK_BLOCK_SIZE)
    causal = lax.broadcasted_iota(jnp.int32, square, 0) >= lax.broadcasted_iota(jnp.int32, square, 1)
    ones = jnp.ones(square, jnp.bfloat16)
    factor = HEAD_SIZE**-0.5 * LOG2E
    own_row = (0 if relay else rank) * chip_rows

    def row_of(block):
        chip = block // cores
        if relay:
            slot = (rank // columns - chip // columns) * columns + jnp.bitwise_xor(rank % columns, chip % columns)
        else:
            slot = chip
        return (slot * cores + jnp.bitwise_xor(block % cores, core)) * MASK_BLOCK_SIZE

    def tile_rows(row):
        return pl.ds(pl.multiple_of(row, MASK_BLOCK_SIZE), MASK_BLOCK_SIZE)

    def product(left, rights):
        return lax.dot_general(
            left, jnp.concatenate(rights, axis=0), (((1,), (1,)), ((), ())), preferred_element_type=jnp.float32
        )

    def weighted(weights, rights):
        right = jnp.concatenate([jnp.concatenate([value, ones], axis=1) for value in rights], axis=0)
        return jnp.dot(weights, right, preferred_element_type=jnp.float32)

    def part(array, index, axis):
        return lax.slice_in_dim(array, index * MASK_BLOCK_SIZE, (index + 1) * MASK_BLOCK_SIZE, axis=axis)

    def results(kv):
        lanes = pl.ds(pl.multiple_of(kv * width, width), width)
        made = []
        if own:
            target = pl.ds(pl.multiple_of((core * half + kv_first + kv) * width, width), width)
            made.append(pltpu.make_async_copy(own_made.at[:, lanes], out.at[:, target], out_sems.at[kv, 0]))
        if sibling:
            made.append(pltpu.make_async_copy(sibling_made.at[:, lanes], sibling_out.at[:, lanes], out_sems.at[kv, 1]))
        return made

    def of_head(kv, carry):
        key_lanes = pl.ds(pl.multiple_of(kv * HEAD_SIZE, HEAD_SIZE), HEAD_SIZE)
        value_lanes = pl.ds(pl.multiple_of((kv_heads + kv) * HEAD_SIZE, HEAD_SIZE), HEAD_SIZE)
        sides = []
        if own:
            sides.append((own_queries, own_made, rank * cores + core, own_row))
        if sibling:
            sides.append((sibling_queries, sibling_made, rank * cores + other, own_row + MASK_BLOCK_SIZE))

        def lanes_of(slot):
            return pl.ds(pl.multiple_of(kv * width + slot * HEAD_SIZE, HEAD_SIZE), HEAD_SIZE)

        def query(held, slot):
            start = (kv_first + kv) * width + slot * HEAD_SIZE
            if held is own_queries:
                start = start + core * half * width
            return held[:, pl.ds(pl.multiple_of(start, HEAD_SIZE), HEAD_SIZE)]

        def key(row):
            return rows_held[tile_rows(row), key_lanes]

        def value(row):
            return rows_held[tile_rows(row), value_lanes]

        diagonal = [
            product(jnp.concatenate([query(held, slot) for slot in range(GROUP)], axis=0), [key(row)])
            for held, _, _, row in sides
        ]
        pending = []
        for slot in range(GROUP):
            head = (core * half + kv_first + kv) * GROUP + slot
            queries = [query(held, slot) for held, _, _, _ in sides]
            verticals = []
            for entry in range(vertical_width):
                vertical = table[vertical_at + head * vertical_width + entry]
                live = entry < table[vertical_count_at + head]
                verticals.append((vertical, live, row_of(jnp.minimum(vertical, rank * cores))))
            vertical_scores = product(jnp.concatenate(queries, axis=0), [key(row) for _, _, row in verticals])
            made = []
            for side, (_, _, block, diagonal_row) in enumerate(sides):
                slashes = []
                for entry in range(slash_width):
                    target = block - table[slash_at + head * slash_width + entry]
                    use = (entry < table[slash_count_at + head]) & (target >= 0)
                    for vertical, live, _ in verticals:
                        use = use & jnp.logical_not(live & (vertical == target))
                    slashes.append((use, row_of(jnp.where(use, target, block))))
                slash_scores = product(queries[side], [key(row) for _, row in slashes])
                tiles = [jnp.where(causal, part(diagonal[side], slot, 0), -jnp.inf)]
                across = part(vertical_scores, side, 0)
                for index, (vertical, live, _) in enumerate(verticals):
                    tiles.append(jnp.where(live & (vertical < block), part(across, index, 1), -jnp.inf))
                for index, (use, _) in enumerate(slashes):
                    tiles.append(jnp.where(use, part(slash_scores, index, 1), -jnp.inf))
                peak = jnp.max(functools.reduce(jnp.maximum, tiles), axis=1, keepdims=True)
                weights = [jnp.exp2((tile - peak) * factor).astype(jnp.bfloat16) for tile in tiles]
                last = 1 + len(verticals)
                total = weighted(jnp.concatenate(weights[last:], axis=1), [value(row) for _, row in slashes])
                made.append((weights[0], jnp.concatenate(weights[1:last], axis=1), total))
            vertical_sums = weighted(
                jnp.concatenate([one[1] for one in made], axis=0), [value(row) for _, _, row in verticals]
            )
            pending.append([(one[0], one[2] + part(vertical_sums, side, 0)) for side, one in enumerate(made)])
        for side, (_, to, _, diagonal_row) in enumerate(sides):
            sums = weighted(jnp.concatenate([one[side][0] for one in pending], axis=0), [value(diagonal_row)])
            for slot in range(GROUP):
                whole = part(sums, slot, 0) + pending[slot][side][1]
                to[:, lanes_of(slot)] = (whole[:, :HEAD_SIZE] / whole[:, HEAD_SIZE:]).astype(jnp.bfloat16)
            results(kv)[side].start()
        return carry

    lax.fori_loop(0, kv_heads, of_head, 0)
    for kv in range(kv_heads):
        for move in results(kv):
            move.wait()


def attend(table, common, kv_first, kv_heads, queries, sibling_queries, pieces, slots, into=None):
    relay, columns, cores, offsets, widths = common
    own, sibling = queries is not None, sibling_queries is not None
    some = queries if own else sibling_queries
    tokens = some.shape[0]
    width = kv_heads * GROUP * HEAD_SIZE
    plan = (relay, columns, cores, kv_first, kv_heads, own, sibling, tuple(slots), offsets, widths, into is not None)
    operands = [array for array in (queries, sibling_queries) if array is not None]
    operands += list(pieces)
    aliases = {}
    if into is not None:
        aliases = {1 + len(operands): 0}
        operands.append(into)
    shapes = []
    if own:
        shapes.append(jax.ShapeDtypeStruct((tokens, QUERY_HEADS * HEAD_SIZE), jnp.bfloat16))
    if sibling:
        shapes.append(jax.ShapeDtypeStruct((tokens, width), jnp.bfloat16))
    anywhere = pl.BlockSpec(memory_space=pl.ANY)
    resident = pl.BlockSpec(memory_space=pltpu.VMEM)
    held = pltpu.VMEM((tokens, width), jnp.bfloat16)
    small = pltpu.VMEM((16, HEAD_SIZE), jnp.bfloat16)
    rows = sum(piece.shape[0] for piece in pieces)
    return pl.pallas_call(
        functools.partial(attend_kernel, plan),
        grid_spec=pltpu.PrefetchScalarGridSpec(
            num_scalar_prefetch=1,
            grid=(),
            in_specs=[resident] * (own + sibling) + [anywhere] * (len(operands) - own - sibling),
            out_specs=[anywhere] * len(shapes),
            scratch_shapes=[pltpu.VMEM((rows, 2 * kv_heads * HEAD_SIZE), jnp.bfloat16)]
            + [held if own else small]
            + [held if sibling else small]
            + [
                pltpu.SemaphoreType.DMA((len(pieces) + 2,)),
                pltpu.SemaphoreType.DMA((kv_heads, 2)),
            ],
        ),
        out_shape=shapes,
        input_output_aliases=aliases,
        name="attend",
        compiler_params=pltpu.CompilerParams(vmem_limit_bytes=4 * rows * kv_heads * HEAD_SIZE + 2**24),
    )(table, *operands)


def shards(queries, keys, values, vertical_blocks, vertical_count, slash_offsets, slash_count):
    tokens = queries.shape[0]
    ranks = lax.axis_size("seq")
    cores = lax.axis_size("tp")
    assert tokens == MASK_BLOCK_SIZE and cores == 2
    rank = lax.axis_index("seq")
    core = lax.axis_index("tp")
    other = cores - 1 - core
    columns = 2
    lines = ranks // columns
    relay = lines == 4
    half = KEY_VALUE_HEADS // cores
    group_width = GROUP * HEAD_SIZE
    swap = [(0, 1), (1, 0)]
    chunks = ((0, half // 2), (half // 2, half - half // 2))

    parts = [vertical_blocks, vertical_count, slash_offsets, slash_count, rank, core]
    sizes = [part.size for part in parts]
    offsets = tuple(sum(sizes[:n]) for n in range(len(sizes)))
    table = jnp.concatenate([part.astype(jnp.int32).reshape(-1) for part in parts])
    common = (relay, columns, cores, offsets, (vertical_blocks.shape[1], slash_offsets.shape[1]))

    def taken(of_core, first, count):
        start = (of_core * half + first) * HEAD_SIZE
        return jnp.concatenate(
            [lax.dynamic_slice_in_dim(array, start, count * HEAD_SIZE, 1) for array in (keys, values)], axis=1
        )

    local = []
    for name, (first, count) in zip("ab", chunks):
        mine, theirs = taken(core, first, count), taken(other, first, count)
        if name == "b":
            mine, theirs = lax.optimization_barrier((mine, theirs))
        got = lax.ppermute(theirs, "tp", swap)
        local.append(jnp.concatenate([mine, got], axis=0))
    sibling_queries = lax.ppermute(
        lax.dynamic_slice_in_dim(queries, other * half * group_width, half * group_width, 1), "tp", swap
    )

    if relay:

        def along(array, step):
            pairs = [
                (line * columns + column, (line + 1) * columns + column)
                for line in range(step - 1, lines - 1)
                for column in range(columns)
            ]
            return lax.ppermute(array, "seq", pairs)

        def across(array, step):
            pairs = [
                (line * columns + column, line * columns + 1 - column)
                for line in range(step, lines)
                for column in range(columns)
            ]
            return lax.ppermute(array, "seq", pairs)

        def from_first(array):
            pairs = [(column, (lines - 1) * columns + column) for column in range(columns)]
            return lax.ppermute(array, "seq", pairs)

        line_slots = [step * columns for step in range(lines)]
        a, b = [local[0]], [local[1]]
        a.append(along(a[0], 1))
        a.append(along(a[1], 2))
        a.append(from_first(a[0]))
        a += [across(a[step], step) for step in range(lines)]
        b.append(along(b[0], 1))
        b.append(along(b[1], 2))
        b += [across(b[step], step) for step in range(lines - 1)]
        both = jnp.concatenate([b[0], b[lines - 1]], axis=0)
        b.append(from_first(both))
        gathered = [a, b]
        slots = [
            line_slots + [slot + 1 for slot in line_slots],
            line_slots[:-1] + [slot + 1 for slot in line_slots[:-1]] + line_slots[-1:],
        ]
    else:
        gathered = [[lax.all_gather(piece, "seq", axis=0, tiled=True)] for piece in local]
        slots = [[0], [0]]

    (first_a, count_a), (first_b, count_b) = chunks
    out, sibling_a = attend(table, common, first_a, count_a, queries, sibling_queries, gathered[0], slots[0])
    got_a = lax.ppermute(sibling_a, "tp", swap)
    out, sibling_b = attend(table, common, first_b, count_b, queries, sibling_queries, gathered[1], slots[1], into=out)
    got_b = lax.ppermute(sibling_b, "tp", swap)
    for got, first in ((got_a, first_a), (got_b, first_b)):
        out = lax.dynamic_update_slice_in_dim(out, got, (other * half + first) * group_width, 1)
    return out


def solution(mesh):
    return jax.shard_map(
        shards,
        mesh=mesh,
        in_specs=(
            P(("groups", "seq", "tp"), None),
            P(("groups", "seq", "tp"), None),
            P(("groups", "seq", "tp"), None),
            P(),
            P(),
            P(),
            P(),
        ),
        out_specs=P(("groups", "seq", "tp"), None),
        check_vma=False,
    )
```
